128 devices in a mesh: lon: 16 (over y, x), lat: 8 (over z, core).
Axes of the slice: x: 4, y: 4, z: 4, core: 2. Of those that a mesh axis runs over, the one named last changes fastest.
Arguments:
- concentration: float32 [72, 8, 128, 2048], P(None, None, 'lat', 'lon'), may hold values from -0.3 to 0.3
- adjoint: float32 [72, 8, 128, 2048], P(None, None, 'lat', 'lon'), may hold values from -4 to 4
- wind_east: float32 [72, 128, 2048], P(None, 'lat', 'lon'), may hold values from -0.45 to 0.45
- wind_north: float32 [72, 128, 2048], P(None, 'lat', 'lon'), may hold values from -0.45 to 0.45
- mixing: float32 [72, 128, 2048], P(None, 'lat', 'lon'), may hold values from 0.01 to 100
- sound_col: int32 [1, 128, 4096], P(None, ('lon', 'lat')), may hold values from -1 to 2047, as said below
- kernel: float32 [72, 128, 4096], P(None, ('lon', 'lat')), may hold values from 0.5 to 3
- observed: float32 [1, 128, 4096], P(None, ('lon', 'lat')), may hold values from -12 to 12
- obs_error: float32 [1, 128, 4096], P(None, ('lon', 'lat')), may hold values from 1 to 3
Outputs:
- adjoint_out: float32 [72, 8, 128, 2048], P(None, None, 'lat', 'lon')
- residual: float32 [1, 128, 4096], P(None, ('lon', 'lat'))
The draws below stay inside these ranges and needn't reach their ends.
Inputs may be any that keep to these rules, and one draw needn't show every extreme that they name: `sound_col`: each entry is a column index inside the brick of its slot (slots b * 32 to b * 32 + 31 of an owner belong to brick b in lon-major order), or -1 for an empty slot; for each owner and brick the used slots come first. In every draw some brick receives 32 soundings from every owner.
All inputs are finite; a program needn't handle non-finite values.
Results may differ from the reference program's by a relative error of at most 0.00022.
Values sent between devices are 32-bit elements; how exact they have to be, the bound alone decides.
A program may use at most 192 MiB of HBM per device.

```python
import math
import jax
import jax.numpy as jnp
from jax import lax

VERTICAL_LEVELS = 72
TR = 8
CX = 128
CY = 16
CAP = 32
BRICKS = 128
SLOTS = 4096
NX = 2048
NY = 128
N_LAT = 8


def draw_sound_col(key, part):
    key_count, key_busy, key_full, key_cols = jax.random.split(jax.random.fold_in(key, 11), 4)
    loaded = jax.random.randint(key_count, (BRICKS, BRICKS), 0, CAP + 1)
    busyness = jnp.left_shift(jnp.int32(1), jax.random.randint(key_busy, (1, BRICKS), 0, 4))
    counts = jnp.minimum(loaded * busyness // 4, CAP)
    fullest = jax.random.randint(key_full, (), 0, BRICKS)
    brick_index = jnp.arange(BRICKS)[None, :]
    counts = jnp.where(brick_index == fullest, CAP, counts)
    columns = jax.random.randint(key_cols, (BRICKS, BRICKS, CAP), 0, CY * CX)
    slot_index = jnp.arange(CAP)[None, None, :]
    picked = jnp.where(slot_index < counts[:, :, None], columns, -1)
    return picked.reshape(1, BRICKS, BRICKS * CAP).astype(jnp.int32)


def draw_mixing(key, part):
    key_kind, key_weak, key_strong, key_level_set, key_cut = jax.random.split(jax.random.fold_in(key, 23), 5)
    share = 0.5
    strong_low = 20.0
    strong = jax.random.uniform(key_kind, (1, NY, NX), jnp.float32) < share
    weak_values = jnp.exp(jax.random.uniform(key_weak, (VERTICAL_LEVELS, NY, NX), jnp.float32, jnp.log(0.05), jnp.log(3.0)))
    strong_values = jnp.exp(jax.random.uniform(key_strong, (VERTICAL_LEVELS, NY, NX), jnp.float32, jnp.log(strong_low), jnp.log(100.0)))
    base = jnp.where(strong, strong_values, weak_values)
    group_levels = jax.random.randint(key_level_set, (3,), 0, VERTICAL_LEVELS)
    level_position = jnp.arange(VERTICAL_LEVELS)[:, None]
    sounding_group = jnp.any(level_position == group_levels[None, :], axis=1).reshape(VERTICAL_LEVELS, 1, 1)
    level_cutoff = jax.random.uniform(key_cut, (1, NY, NX), jnp.float32, 0.2, 0.5)
    weight_factor = jnp.where(sounding_group, level_cutoff, 1.0)
    return (base * weight_factor).astype(jnp.float32)


def draw_adjoint(key, part):
    key_rough, key_common = jax.random.split(jax.random.fold_in(key, 37), 2)
    rough = 0.8 * jax.random.normal(key_rough, (VERTICAL_LEVELS, TR, NY, NX), jnp.float32)
    common = 0.6 * jax.random.normal(key_common, (1, TR, NY, NX), jnp.float32)
    return jnp.clip(rough + common, -4.0, 4.0).astype(jnp.float32)


def levels(own_key, extent, cuts, low, largest):
    factor_of = 1.0
    for axis_at, shards_of in cuts:
        draws = jax.random.uniform(jax.random.fold_in(jax.random.fold_in(own_key, 6), axis_at), (shards_of,), jnp.float32, low / len(cuts), largest / len(cuts))
        factor_of = factor_of * jnp.repeat(jnp.exp(draws), extent[axis_at] // shards_of).reshape((-1,) + (1,) * (len(extent) - 1 - axis_at))
    return factor_of


def centred(rng, dims, width, limit, shards=(), held_as=jnp.bfloat16):
    drawn = width * jax.random.normal(rng, dims, jnp.float32)
    if shards:
        drawn = drawn * levels(rng, dims, shards, -0.22, 0.18)
    return jnp.clip(drawn, -limit, limit).astype(held_as)


def setup_inputs(seed: int = 0) -> dict:
    seeds = jax.random.split(jax.random.key(seed), 10)
    return {
        "concentration": centred(seeds[0], (VERTICAL_LEVELS, TR, NY, NX), 0.05, 0.3, ((2, 8), (3, 16)), jnp.float32),
        "adjoint": draw_adjoint(jax.random.fold_in(seeds[9], 71), 0),
        "wind_east": jnp.clip(jax.random.uniform(seeds[2], (VERTICAL_LEVELS, NY, NX), jnp.float32, -0.45, 0.45) * levels(seeds[2], (VERTICAL_LEVELS, NY, NX), ((1, 8), (2, 16)), -0.4, 0.0), -0.45, 0.45),
        "wind_north": jnp.clip(jax.random.uniform(seeds[3], (VERTICAL_LEVELS, NY, NX), jnp.float32, -0.45, 0.45) * levels(seeds[3], (VERTICAL_LEVELS, NY, NX), ((1, 8), (2, 16)), -0.4, 0.0), -0.45, 0.45),
        "mixing": draw_mixing(jax.random.fold_in(seeds[9], 71), 0),
        "sound_col": draw_sound_col(jax.random.fold_in(seeds[9], 71), 0),
        "kernel": jnp.clip(jnp.exp(math.log(3.0) - 1.7917595 * jax.random.uniform(seeds[6], (VERTICAL_LEVELS, BRICKS, SLOTS), jnp.float32) ** levels(seeds[6], (VERTICAL_LEVELS, BRICKS, SLOTS), ((1, 128),), -0.2, 0.2)), 0.5, 3.0),
        "observed": centred(seeds[7], (1, BRICKS, SLOTS), 2.0, 12.0, ((1, 128),), jnp.float32),
        "obs_error": jnp.clip(jnp.exp(math.log(3.0) - 1.0986123 * jax.random.uniform(seeds[8], (1, BRICKS, SLOTS), jnp.float32) ** levels(seeds[8], (1, BRICKS, SLOTS), ((1, 128),), -0.2, 0.2)), 1.0, 3.0),
    }


def advect(padded, east_wind, north_wind):
    centre = padded[..., 1:-1, 1:-1]
    eastern = padded[..., 1:-1, 2:]
    western = padded[..., 1:-1, :-2]
    northern = padded[..., 2:, 1:-1]
    southern = padded[..., :-2, 1:-1]
    out_east = jnp.maximum(east_wind[:, 1:-1, 1:-1], 0.0)[:, None]
    in_west = jnp.minimum(east_wind[:, 1:-1, :-2], 0.0)[:, None]
    out_north = jnp.maximum(north_wind[:, 1:-1, 1:-1], 0.0)[:, None]
    in_south = jnp.minimum(north_wind[:, :-2, 1:-1], 0.0)[:, None]
    staying = 1.0 - out_east + in_west - out_north + in_south
    return centre * staying + out_east * eastern - in_west * western + out_north * northern - in_south * southern


def diffuse(field, mixing):
    level_count = field.shape[0]
    level_position = lax.broadcasted_iota(jnp.int32, mixing.shape, 0)
    upward = jnp.where(level_position < level_count - 1, mixing, 0.0)
    downward = jnp.concatenate([jnp.zeros_like(upward[:1]), upward[:-1]], axis=0)
    middle = 1.0 + upward + downward

    def sweep_down(running, inputs):
        weight_factor, solved = running
        below_term, centre_term, above_term, source = inputs
        pivot_term = centre_term - below_term * weight_factor
        next_factor = above_term / pivot_term
        next_value = (source + below_term[None] * solved) / pivot_term[None]
        return (next_factor, next_value), (next_factor, next_value)

    initial = (jnp.zeros_like(mixing[0]), jnp.zeros_like(field[0]))
    ignored, (factors, values) = lax.scan(sweep_down, initial, (downward, middle, upward, field))

    def sweep_up(running, inputs):
        weight_factor, solved = inputs
        result = solved + weight_factor[None] * running
        return result, result

    ignored, finished = lax.scan(sweep_up, jnp.zeros_like(field[0]), (factors, values), reverse=True)
    return finished


def pad_rims(field):
    wrapped = jnp.concatenate([field[..., -1:], field, field[..., :1]], axis=-1)
    widths = [(0, 0)] * (field.ndim - 2) + [(1, 1), (0, 0)]
    return jnp.pad(wrapped, widths)


def reference(concentration, adjoint, wind_east, wind_north, mixing, sound_col, kernel, observed, obs_error):
    profile_sum = jnp.sum(concentration, axis=1).reshape(VERTICAL_LEVELS, NY * NX)
    columns = sound_col[0]
    brick_index = lax.broadcasted_iota(jnp.int32, columns.shape, 1) // CAP
    cell_index = jnp.maximum(columns, 0)
    grid_row = (brick_index % N_LAT) * CY + cell_index // CX
    grid_col = (brick_index // N_LAT) * CX + cell_index % CX
    flat_index = (grid_row * NX + grid_col).reshape(-1).astype(jnp.int32)
    sampled = profile_sum[:, flat_index].reshape(VERTICAL_LEVELS, BRICKS, SLOTS)
    modelled = jnp.sum(kernel * sampled, axis=0, keepdims=True)
    residual = jnp.where(sound_col >= 0, (modelled - observed) / obs_error, 0.0)
    weights = kernel * (residual / obs_error)
    forcing_cols = jnp.zeros((VERTICAL_LEVELS, NY * NX), jnp.float32).at[:, flat_index].add(weights.reshape(VERTICAL_LEVELS, -1))
    started = adjoint + forcing_cols.reshape(VERTICAL_LEVELS, 1, NY, NX)
    east_pad = pad_rims(wind_east)
    north_pad = pad_rims(wind_north)

    def two_steps(tracer_field):
        single = tracer_field[:, None]
        stepped = diffuse(advect(pad_rims(single), east_pad, north_pad), mixing)
        finished = diffuse(advect(pad_rims(stepped), east_pad, north_pad), mixing)
        return finished[:, 0]

    adjoint_out = jnp.moveaxis(lax.map(two_steps, jnp.moveaxis(started, 1, 0)), 0, 1)
    return adjoint_out, residual
```

```python
import functools

import jax
import jax.numpy as jnp
from jax import lax
from jax.experimental import pallas as pl
from jax.experimental.pallas import tpu as pltpu
from jax.sharding import PartitionSpec as P

MESH = pl.DeviceIdType.MESH
LANES = 128
ROWS = 16
TRACERS = 8
BLOCK = TRACERS * ROWS
F32 = jnp.float32
BF16 = jnp.bfloat16


def lane_ids(rows):
    return lax.broadcasted_iota(jnp.int32, (rows, LANES), 1)


def row_ids(rows):
    return lax.broadcasted_iota(jnp.int32, (rows, LANES), 0)


def swap_blocks(v, lane):
    low = lane < 64
    even = (lane // 32) % 2 == 0
    out = []
    first = [None] * 4
    for b in range(2):
        first[b] = jnp.where(low, v[b], pltpu.roll(v[2 + b], 64, 1))
        first[2 + b] = jnp.where(low, pltpu.roll(v[b], 64, 1), v[2 + b])
    for h in range(2):
        a, b = first[2 * h], first[2 * h + 1]
        out.append(jnp.where(even, a, pltpu.roll(b, 32, 1)))
        out.append(jnp.where(even, pltpu.roll(a, 96, 1), b))
    return out


def pack_lon(src, blocks, dst):
    lane = lane_ids(8)
    pair = ((lane + 127) % 128) // 2

    def group(g, count):
        acc = jnp.zeros((8, LANES), F32)
        for kk in range(count):
            for j in range(16):
                slot = kk * 16 + j
                v = src[pl.ds(pl.multiple_of((g * 4 + kk) * BLOCK + j * 8, 8), 8), :]
                acc = jnp.where(pair == slot, pltpu.roll(v, (2 * slot + 2) % LANES, 1), acc)
        dst[pl.ds(pl.multiple_of(g * 8, 8), 8), :] = acc

    def body(g, c):
        group(g, 4)
        return c

    lax.fori_loop(0, blocks // 4, body, 0)
    if blocks % 4:
        group(blocks // 4, blocks % 4)


def pack_lat(src, blocks, row, dst):
    def body(k, c):
        dst[pl.ds(pl.multiple_of(k * 8, 8), 8), :] = src[pl.ds(k * BLOCK + row, 8, stride=ROWS), :]
        return c

    lax.fori_loop(0, blocks, body, 0, unroll=3)


def merge_lon(west, east, groups, dst):
    odd = lane_ids(8) % 2 == 1

    def body(g, c):
        rows = pl.ds(pl.multiple_of(g * 8, 8), 8)
        dst[rows, :] = jnp.where(odd, west[rows, :], pltpu.roll(east[rows, :], 126, 1))
        return c

    lax.fori_loop(0, groups, body, 0)


def outer_columns(merged, block, j):
    rows = pl.ds(pl.multiple_of((block // 4) * 8, 8), 8)
    v = merged[rows, :]
    slot = lax.rem(block, 4) * 16 + 2 * j
    return jnp.concatenate(
        [pltpu.roll(v, LANES - 1 - 2 * slot, 1), pltpu.roll(v, LANES - 3 - 2 * slot, 1)], axis=0
    )


def transport(field, levels, tracers, merged, south, north, coef):
    lane = lane_ids(ROWS)
    row = row_ids(ROWS)
    first_lane, last_lane = lane == 0, lane == LANES - 1
    first_row, last_row = row == 0, row == ROWS - 1
    c0, ce, cw, cn, cs, ca, cg = coef

    def down(block, j, level, above):
        at = pl.multiple_of(block * BLOCK + j * ROWS, 8)
        v = field[pl.ds(at, ROWS), :]
        cols = outer_columns(merged, block, j)
        edge = block * 8 + j
        lo = jnp.broadcast_to(south[pl.ds(edge, 1), :], (ROWS, LANES))
        hi = jnp.broadcast_to(north[pl.ds(edge, 1), :], (ROWS, LANES))
        east = jnp.where(last_lane, cols, pltpu.roll(v, LANES - 1, 1))
        west = jnp.where(first_lane, cols, pltpu.roll(v, 1, 1))
        up = jnp.where(last_row, hi, pltpu.roll(v, ROWS - 1, 0))
        dn = jnp.where(first_row, lo, pltpu.roll(v, 1, 0))
        new = level[0] * v + level[1] * east + level[2] * west + level[3] * up + level[4] * dn + level[5] * above
        field[pl.ds(at, ROWS), :] = new
        return new

    def at_level(k, refs):
        rows = pl.ds(pl.multiple_of(k * ROWS, ROWS), ROWS)
        return [ref[rows, :] for ref in refs]

    if tracers == TRACERS:

        def down_body(k, carry):
            level = at_level(k, (c0, ce, cw, cn, cs, ca))
            return tuple(down(k, t, level, carry[t]) for t in range(TRACERS))

        zero = jnp.zeros((ROWS, LANES), F32)
        last = lax.fori_loop(0, levels, down_body, (zero,) * TRACERS)

        def up_body(i, carry):
            k = levels - 2 - i
            g = at_level(k, (cg,))[0]
            out = []
            for t in range(TRACERS):
                rows = pl.ds(pl.multiple_of(k * BLOCK + t * ROWS, 8), ROWS)
                new = field[rows, :] + g * carry[t]
                field[rows, :] = new
                out.append(new)
            return tuple(out)

        lax.fori_loop(0, levels - 1, up_body, last)
    else:

        def down_one(a, carry):
            for b in range(8):
                carry = down(a, b, at_level(a * 8 + b, (c0, ce, cw, cn, cs, ca)), carry)
            return carry

        last = lax.fori_loop(0, levels // 8, down_one, jnp.zeros((ROWS, LANES), F32))

        def up_one(i, carry):
            for b in range(8):
                k = levels - 1 - (i * 8 + b)
                rows = pl.ds(pl.multiple_of(k * ROWS, ROWS), ROWS)
                carry = field[rows, :] + cg[rows, :] * carry
                field[rows, :] = carry
            return carry

        lax.fori_loop(0, levels // 8, up_one, jnp.zeros((ROWS, LANES), F32))


def window_kernel(
    n_lon, n_lat, levels,
    conc_hbm, adj_hbm, we_hbm, wn_hbm, mix_hbm, col_hbm, kern_hbm, obs_hbm, err_hbm,
    adj_out, force_out, res_out,
    field, conc, we, wn, mix, prof, force, c0, ce, cw, cn, cs, ca, cg,
    kv, colv, obsv, errv, sendb, recvb, kn, coln, wres, resb,
    lhs, rhs,
    q_adj0, q_adj1, q_one, lat_a, lat_b, lat_one_a, lat_one_b,
    w_adj0, e_adj0, w_adj1, e_adj1, s_adj0, n_adj0, s_adj1, n_adj1,
    w_one, e_one, s_one, n_one, m_adj, m_one,
    load_sem, out_sem, a2a_send, a2a_recv, res_send, res_recv, self_sem, halo_send, halo_recv, stage_sem,
):
    lon, lat = lax.axis_index("lon"), lax.axis_index("lat")
    bricks = n_lon * n_lat
    me = lon * n_lat + lat
    per = levels // 4 + 1
    tiles = bricks // 4
    groups = tiles // 8

    loads = [
        (kern_hbm, kv), (col_hbm, colv), (obs_hbm, obsv), (err_hbm, errv), (we_hbm, we), (wn_hbm, wn),
        (adj_hbm, field), (mix_hbm, mix), (conc_hbm, conc),
    ]
    loads = [pltpu.make_async_copy(a, b, load_sem.at[i]) for i, (a, b) in enumerate(loads)]
    for copy in loads:
        copy.start()

    barrier = pltpu.get_barrier_semaphore()
    for d in range(1, n_lat):
        pl.semaphore_signal(barrier, inc=1, device_id=(lon, lax.rem(lat + d, n_lat)), device_id_type=MESH)
    for d in range(1, n_lon):
        pl.semaphore_signal(barrier, inc=1, device_id=(lax.rem(lon + d, n_lon), lat), device_id_type=MESH)

    lane8 = lane_ids(8)
    for i in range(4):
        loads[i].wait()

    def pack_rows(kk, c, v):
        y = swap_blocks(v, lane8)
        for m in range(4):
            sendb[pl.ds((c * 32 + m) * per + kk, 8, stride=4 * per), :] = y[m]

    def pack_body(kk, carry):
        for c in range(groups):
            pack_rows(kk, c, [kv[pl.ds(pl.multiple_of((kk * 4 + q) * tiles + c * 8, 8), 8), :] for q in range(4)])
        return carry

    lax.fori_loop(0, levels // 4, pack_body, 0)
    for c in range(groups):
        rows = pl.ds(c * 8, 8)
        e = errv[rows, :]
        pack_rows(levels // 4, c, [colv[rows, :].astype(F32), obsv[rows, :], e, e])

    loads[4].wait()
    loads[5].wait()
    pack_lon(we, levels // 8, q_one.at[0])
    pack_lat(wn, levels // 8, ROWS - 1, lat_one_a.at[0])
    loads[6].wait()
    pack_lon(field, levels, q_adj0)
    pack_lat(field, levels, ROWS - 1, lat_a.at[0])
    pack_lat(field, levels, 0, lat_b.at[0])

    pl.semaphore_wait(barrier, n_lon + n_lat - 2)
    for d in range(1, n_lat):
        pl.semaphore_signal(stage_sem, inc=1, device_id=(lon, lax.rem(lat + d, n_lat)), device_id_type=MESH)
    pl.semaphore_wait(stage_sem, n_lat - 1)

    east = (lax.rem(lon + 1, n_lon), lat)
    west = (lax.rem(lon + n_lon - 1, n_lon), lat)
    north = (lon, lax.rem(lat + 1, n_lat))
    south = (lon, lax.rem(lat + n_lat - 1, n_lat))

    def remote(src, dst, index, device):
        return pltpu.make_async_remote_copy(
            src, dst, halo_send.at[index], halo_recv.at[index], device_id=device, device_id_type=MESH
        )

    def exchange(first, q, top, bottom, w, e, s, n):
        copies = [
            remote(top, s, first, north), remote(bottom, n, first + 1, south),
            remote(q, w, first + 2, east), remote(q, e, first + 3, west),
        ]
        for copy in copies:
            copy.start()
        return copies

    def land(copies):
        for copy in copies:
            copy.wait()

    wind_copies = [
        remote(q_one.at[0], w_one.at[0], 0, east), remote(lat_one_a.at[0], s_one.at[0], 1, north),
    ]
    for copy in wind_copies:
        copy.start()
    halo = exchange(2, q_adj0, lat_a.at[0], lat_b.at[0], w_adj0, e_adj0, s_adj0, n_adj0)

    def peer(i):
        d = lax.rem(i * 37, bricks)
        tl, ta = lax.rem(lon + d // n_lat, n_lon), lax.rem(lat + lax.rem(d, n_lat), n_lat)
        return tl, ta, tl * n_lat + ta

    def send_body(i, c):
        tl, ta, t = peer(i)
        pltpu.make_async_remote_copy(
            sendb.at[pl.ds(t * per, per)], recvb.at[pl.ds(me * per, per)], a2a_send, a2a_recv,
            device_id=(tl, ta), device_id_type=MESH,
        ).start()
        return c

    lax.fori_loop(1, bricks, send_body, 0)
    own = pltpu.make_async_copy(sendb.at[pl.ds(me * per, per)], recvb.at[pl.ds(me * per, per)], self_sem)
    own.start()

    loads[7].wait()
    loads[8].wait()

    def tracer_sum(k, c):
        total = conc[pl.ds(pl.multiple_of(k * BLOCK, 8), ROWS), :]
        for t in range(1, TRACERS):
            total = total + conc[pl.ds(pl.multiple_of(k * BLOCK + t * ROWS, 8), ROWS), :]
        prof[pl.ds(pl.multiple_of(k * ROWS, 8), ROWS), :] = total
        return c

    lax.fori_loop(0, levels, tracer_sum, 0, unroll=2)

    land(wind_copies)
    lane = lane_ids(ROWS)
    row = row_ids(ROWS)
    merge_lon(w_one.at[0], w_one.at[0], (levels // 8 + 3) // 4, m_one)
    southmost = lat == 0
    northmost = lat == n_lat - 1
    open_north = jnp.logical_not(jnp.logical_and(row == ROWS - 1, northmost)).astype(F32)
    open_south = jnp.where(southmost, 0.0, 1.0)

    def coefficients(a, carry):
        above, factor = carry
        for b in range(8):
            k = a * 8 + b
            rows = pl.ds(pl.multiple_of(k * ROWS, ROWS), ROWS)
            u, n = we[rows, :], wn[rows, :]
            cols = outer_columns(m_one, a, b)
            u_west = jnp.where(lane == 0, cols, pltpu.roll(u, 1, 1))
            edge = jnp.broadcast_to(s_one[0, pl.ds(k, 1), :], (ROWS, LANES)) * open_south
            n_south = jnp.where(row == 0, edge, pltpu.roll(n, 1, 0))
            ep, wm = jnp.maximum(u, 0.0), jnp.minimum(u_west, 0.0)
            up, sm = jnp.maximum(n, 0.0), jnp.minimum(n_south, 0.0)
            below = mix[rows, :] * jnp.where(k < levels - 1, 1.0, 0.0)
            inv = 1.0 / (1.0 + below + above - above * factor)
            c0[rows, :] = (1.0 - ep + wm - up + sm) * inv
            ce[rows, :] = ep * inv
            cw[rows, :] = -wm * inv
            cn[rows, :] = up * open_north * inv
            cs[rows, :] = -sm * inv
            ca[rows, :] = above * inv
            factor = below * inv
            cg[rows, :] = factor
            above = below
        return above, factor

    zero = jnp.zeros((ROWS, LANES), F32)
    lax.fori_loop(0, levels // 8, coefficients, (zero, zero))
    coef = (c0, ce, cw, cn, cs, ca, cg)

    land(halo)
    merge_lon(w_adj0, e_adj0, levels // 4, m_adj)
    transport(field, levels, TRACERS, m_adj, s_adj0, n_adj0, coef)
    pack_lon(field, levels, q_adj1)
    pack_lat(field, levels, ROWS - 1, lat_a.at[1])
    pack_lat(field, levels, 0, lat_b.at[1])
    halo = exchange(6, q_adj1, lat_a.at[1], lat_b.at[1], w_adj1, e_adj1, s_adj1, n_adj1)
    land(halo)
    merge_lon(w_adj1, e_adj1, levels // 4, m_adj)
    transport(field, levels, TRACERS, m_adj, s_adj1, n_adj1, coef)
    adj_copy = pltpu.make_async_copy(field, adj_out, out_sem.at[0])
    adj_copy.start()

    own.wait()
    rest = pl.ds(0, (bricks - 1) * per)
    pltpu.make_async_copy(recvb.at[rest], recvb.at[rest], a2a_recv).wait()

    def unpack(kk, c):
        z = [recvb[pl.ds((c * 32 + m) * per + kk, 8, stride=4 * per), :] for m in range(4)]
        return swap_blocks(z, lane8)

    def unpack_body(kk, carry):
        for c in range(groups):
            v = unpack(kk, c)
            for q in range(4):
                kn[pl.ds(pl.multiple_of((kk * 4 + q) * tiles + c * 8, 8), 8), :] = v[q]
        return carry

    lax.fori_loop(0, levels // 4, unpack_body, 0)
    aux = [unpack(levels // 4, c) for c in range(groups)]
    cols = [aux[c][0].astype(jnp.int32) for c in range(groups)]
    spots = [lax.bitwise_and(v, LANES - 1) for v in cols]
    bits = [[lax.bitwise_and(v, LANES << b) != 0 for b in range(4)] for v in cols]

    def gather_body(k, acc):
        rows = [
            jnp.broadcast_to(prof[pl.ds(k * ROWS + r, 1), :], (8, LANES)) for r in range(ROWS)
        ]
        out = []
        for c in range(groups):
            picked = [jnp.take_along_axis(v, spots[c], axis=1, mode="promise_in_bounds") for v in rows]
            for b in range(4):
                picked = [jnp.where(bits[c][b], picked[2 * i + 1], picked[2 * i]) for i in range(len(picked) // 2)]
            out.append(acc[c] + kn[pl.ds(pl.multiple_of(k * tiles + c * 8, 8), 8), :] * picked[0])
        return tuple(out)

    modelled = lax.fori_loop(0, levels, gather_body, (jnp.zeros((8, LANES), F32),) * groups)
    for c in range(groups):
        rows = pl.ds(c * 8, 8)
        res = jnp.where(cols[c] >= 0, (modelled[c] - aux[c][1]) / aux[c][2], 0.0)
        wres[rows, :] = res
        coln[rows, :] = cols[c]
        obsv[rows, :] = res / aux[c][2]

    def res_body(i, c):
        tl, ta, t = peer(i)
        pltpu.make_async_remote_copy(
            wres.at[pl.ds(t // 4, 1)], resb.at[pl.ds(me, 1)], res_send, res_recv,
            device_id=(tl, ta), device_id_type=MESH,
        ).start()
        return c

    lax.fori_loop(1, bricks, res_body, 0)
    own_res = pltpu.make_async_copy(wres.at[pl.ds(me // 4, 1)], resb.at[pl.ds(me, 1)], self_sem)
    own_res.start()

    def weigh(k, c):
        for g in range(groups):
            rows = pl.ds(pl.multiple_of(k * tiles + g * 8, 8), 8)
            kn[rows, :] = kn[rows, :] * obsv[pl.ds(g * 8, 8), :]
        return c

    lax.fori_loop(0, levels, weigh, 0)

    cell = lax.broadcasted_iota(jnp.int32, (2 * LANES, LANES), 0)

    def build(c, carry):
        lanes = pl.ds(pl.multiple_of(c * LANES, LANES), LANES)
        w = kn[pl.ds(c, levels, stride=tiles), :]
        high = w.astype(BF16)
        low = (w - high.astype(F32)).astype(BF16)
        lhs[pl.ds(0, levels), lanes] = high
        lhs[pl.ds(levels, levels), lanes] = low
        col = jnp.broadcast_to(coln[pl.ds(c, 1), :], (2 * LANES, LANES))
        rhs[:, lanes] = jnp.where(lax.bitwise_and(col, 2 * LANES - 1) == cell, 1.0, 0.0).astype(BF16)
        return carry

    lax.fori_loop(0, tiles, build, 0)
    colrow = jnp.concatenate([coln[pl.ds(c, 1), :] for c in range(tiles)], axis=1)

    def scatter(r, carry):
        mine = jnp.where(lax.shift_right_arithmetic(colrow, 8) == r, 1.0, 0.0).astype(BF16)
        out = lax.dot_general(
            lhs[...] * mine, rhs[...], (((1,), (1,)), ((), ())), preferred_element_type=F32
        )
        both = out[:levels] + out[levels:]
        force[pl.ds(2 * r, levels, stride=ROWS), :] = both[:, :LANES]
        force[pl.ds(2 * r + 1, levels, stride=ROWS), :] = both[:, LANES:]
        return carry

    lax.fori_loop(0, ROWS // 2, scatter, 0)

    for step in (1, 2):
        pack_lon(force, levels // 8, q_one.at[step])
        pack_lat(force, levels // 8, ROWS - 1, lat_one_a.at[step])
        pack_lat(force, levels // 8, 0, lat_one_b.at[step])
        halo = exchange(
            6 + 4 * step, q_one.at[step], lat_one_a.at[step], lat_one_b.at[step],
            w_one.at[step], e_one.at[step], s_one.at[step], n_one.at[step],
        )
        land(halo)
        merge_lon(w_one.at[step], e_one.at[step], (levels // 8 + 3) // 4, m_one)
        transport(force, levels, 1, m_one, s_one.at[step], n_one.at[step], coef)
    force_copy = pltpu.make_async_copy(force, force_out, out_sem.at[1])
    force_copy.start()

    own_res.wait()
    rest_res = pl.ds(0, bricks - 1)
    pltpu.make_async_copy(resb.at[rest_res], resb.at[rest_res], res_recv).wait()
    mine_block = lax.rem(me, 4)
    for g in range(groups):
        total = jnp.zeros((8, LANES), F32)
        for m in range(4):
            v = resb[pl.ds(g * 32 + m, 8, stride=4), :]
            shift = lax.rem((m - mine_block + 4) * 32, LANES)
            total = jnp.where(lane8 // 32 == m, pltpu.roll(v, shift, 1), total)
        errv[pl.ds(g * 8, 8), :] = total
    res_copy = pltpu.make_async_copy(errv, res_out, out_sem.at[2])
    res_copy.start()

    pltpu.make_async_copy(recvb.at[rest], recvb.at[rest], a2a_send).wait()
    pltpu.make_async_copy(resb.at[rest_res], resb.at[rest_res], res_send).wait()
    adj_copy.wait()
    force_copy.wait()
    res_copy.wait()


def add_kernel(field, force, res, out, res_out):
    for k in range(8):
        one = force[k * ROWS : (k + 1) * ROWS, :]
        for t in range(TRACERS):
            rows = pl.ds(k * BLOCK + t * ROWS, ROWS)
            out[rows, :] = field[rows, :] + one
    res_out[...] = res[...]


def per_device(n_lon, n_lat, concentration, adjoint, wind_east, wind_north, mixing, sound_col, kernel, observed, obs_error):
    levels, tracers, row_count, col_count = adjoint.shape
    bricks = n_lon * n_lat
    slots = sound_col.shape[2]
    tiles = slots // LANES
    per = levels // 4 + 1
    big, one = (levels * BLOCK, LANES), (levels * ROWS, LANES)
    q_rows, q_one_rows = levels // 4 * 8, (levels // 8 + 3) // 4 * 8
    hbm = pl.BlockSpec(memory_space=pl.ANY)
    vm = lambda *shape: pltpu.VMEM(shape, F32)
    scratch = (
        [vm(*big), vm(*big)] + [vm(*one)] * 12
        + [vm(levels * tiles, LANES), pltpu.VMEM((tiles, LANES), jnp.int32), vm(tiles, LANES), vm(tiles, LANES)]
        + [vm(bricks * per, LANES), vm(bricks * per, LANES), vm(levels * tiles, LANES)]
        + [pltpu.VMEM((tiles, LANES), jnp.int32), vm(tiles, LANES), vm(bricks, LANES)]
        + [pltpu.VMEM((2 * levels, slots), BF16), pltpu.VMEM((2 * LANES, slots), BF16)]
        + [vm(q_rows, LANES), vm(q_rows, LANES), vm(3, q_one_rows, LANES)]
        + [vm(2, levels * 8, LANES), vm(2, levels * 8, LANES), vm(3, levels, LANES), vm(3, levels, LANES)]
        + [vm(q_rows, LANES)] * 4 + [vm(levels * 8, LANES)] * 4
        + [vm(3, q_one_rows, LANES), vm(3, q_one_rows, LANES), vm(3, levels, LANES), vm(3, levels, LANES)]
        + [vm(q_rows, LANES), vm(q_one_rows, LANES)]
        + [pltpu.SemaphoreType.DMA((9,)), pltpu.SemaphoreType.DMA((3,))]
        + [pltpu.SemaphoreType.DMA] * 5
        + [pltpu.SemaphoreType.DMA((18,)), pltpu.SemaphoreType.DMA((18,)), pltpu.SemaphoreType.REGULAR]
    )
    field, force, res = pl.pallas_call(
        functools.partial(window_kernel, n_lon, n_lat, levels),
        out_shape=(
            jax.ShapeDtypeStruct(big, F32), jax.ShapeDtypeStruct(one, F32), jax.ShapeDtypeStruct((tiles, LANES), F32),
        ),
        in_specs=[hbm] * 9,
        out_specs=(hbm,) * 3,
        scratch_shapes=scratch,
        compiler_params=pltpu.CompilerParams(collective_id=0, has_side_effects=True, vmem_limit_bytes=48 << 20),
        name="window",
    )(
        concentration.reshape(big), adjoint.reshape(big), wind_east.reshape(one), wind_north.reshape(one),
        mixing.reshape(one), sound_col.reshape(tiles, LANES), kernel.reshape(levels * tiles, LANES),
        observed.reshape(tiles, LANES), obs_error.reshape(tiles, LANES),
    )
    out, residual = pl.pallas_call(
        add_kernel,
        grid=(levels // 8,),
        out_shape=(jax.ShapeDtypeStruct(big, F32), jax.ShapeDtypeStruct((tiles, LANES), F32)),
        in_specs=[
            pl.BlockSpec((8 * BLOCK, LANES), lambda i: (i, 0)),
            pl.BlockSpec((8 * ROWS, LANES), lambda i: (i, 0)),
            pl.BlockSpec((tiles, LANES), lambda i: (0, 0)),
        ],
        out_specs=(pl.BlockSpec((8 * BLOCK, LANES), lambda i: (i, 0)), pl.BlockSpec((tiles, LANES), lambda i: (0, 0))),
        name="combine",
    )(field, force, res)
    return out.reshape(adjoint.shape), residual.reshape(observed.shape)


def solution(mesh):
    in_specs = (
        P(None, None, "lat", "lon"),
        P(None, None, "lat", "lon"),
        P(None, "lat", "lon"),
        P(None, "lat", "lon"),
        P(None, "lat", "lon"),
        P(None, ("lon", "lat"), None),
        P(None, ("lon", "lat"), None),
        P(None, ("lon", "lat"), None),
        P(None, ("lon", "lat"), None),
    )
    out_specs = (P(None, None, "lat", "lon"), P(None, ("lon", "lat"), None))
    return jax.shard_map(
        functools.partial(per_device, mesh.shape["lon"], mesh.shape["lat"]),
        mesh=mesh, in_specs=in_specs, out_specs=out_specs, check_vma=False,
    )
```

```python
import functools

import jax
import jax.numpy as jnp
from jax import lax
from jax.experimental import pallas as pl
from jax.experimental.pallas import tpu as pltpu
from jax.sharding import PartitionSpec as P

MESH = pl.DeviceIdType.MESH
LANES = 128
ROWS = 16
TRACERS = 8
BLOCK = TRACERS * ROWS
COMBINE = 8
UNROLL = 8
F32 = jnp.float32
BF16 = jnp.bfloat16


def lane_ids(rows):
    return lax.broadcasted_iota(jnp.int32, (rows, LANES), 1)


def row_ids(rows):
    return lax.broadcasted_iota(jnp.int32, (rows, LANES), 0)


def swap_blocks(v, lane):
    low = lane < 64
    even = (lane // 32) % 2 == 0
    out = []
    first = [None] * 4
    for b in range(2):
        first[b] = jnp.where(low, v[b], pltpu.roll(v[2 + b], 64, 1))
        first[2 + b] = jnp.where(low, pltpu.roll(v[b], 64, 1), v[2 + b])
    for h in range(2):
        a, b = first[2 * h], first[2 * h + 1]
        out.append(jnp.where(even, a, pltpu.roll(b, 32, 1)))
        out.append(jnp.where(even, pltpu.roll(a, 96, 1), b))
    return out


def pack_lon(src, blocks, dst):
    pair = ((lane_ids(8) + 127) % 128) // 2
    bits = [lax.bitwise_and(pair, 1 << b) != 0 for b in range(6)]

    def tree(parts, level):
        while len(parts) > 1:
            parts = [jnp.where(bits[level], parts[2 * i + 1], parts[2 * i]) for i in range(len(parts) // 2)]
            level += 1
        return parts[0]

    def group(g, count):
        blocks_out = []
        for kk in range(count):
            parts = []
            for j in range(16):
                v = src[pl.ds(pl.multiple_of((g * 4 + kk) * BLOCK + j * 8, 8), 8), :]
                parts.append(pltpu.roll(v, (2 * (kk * 16 + j) + 2) % LANES, 1))
            blocks_out.append(tree(parts, 0))
        blocks_out = (blocks_out * 4)[:4] if count < 4 else blocks_out
        dst[pl.ds(pl.multiple_of(g * 8, 8), 8), :] = tree(blocks_out, 4)

    def body(g, c):
        group(g, 4)
        return c

    lax.fori_loop(0, blocks // 4, body, 0)
    if blocks % 4:
        group(blocks // 4, blocks % 4)


def pack_lat(src, blocks, row, dst):
    def body(k, c):
        dst[pl.ds(pl.multiple_of(k * 8, 8), 8), :] = src[pl.ds(k * BLOCK + row, 8, stride=ROWS), :]
        return c

    lax.fori_loop(0, blocks, body, 0, unroll=3)


def merge_lon(west, east, groups, dst):
    odd = lane_ids(8) % 2 == 1

    def body(g, c):
        rows = pl.ds(pl.multiple_of(g * 8, 8), 8)
        dst[rows, :] = jnp.where(odd, west[rows, :], pltpu.roll(east[rows, :], 126, 1))
        return c

    lax.fori_loop(0, groups, body, 0)


def outer_columns(merged, block, j):
    rows = pl.ds(pl.multiple_of((block // 4) * 8, 8), 8)
    v = merged[rows, :]
    slot = lax.rem(block, 4) * 16 + 2 * j
    return jnp.concatenate(
        [pltpu.roll(v, LANES - 1 - 2 * slot, 1), pltpu.roll(v, LANES - 3 - 2 * slot, 1)], axis=0
    )


def transport(field, levels, which, merged, south, north, coef):
    lane = lane_ids(ROWS)
    row = row_ids(ROWS)
    first_lane, last_lane = lane == 0, lane == LANES - 1
    first_row, last_row = row == 0, row == ROWS - 1
    c0, ce, cw, cn, cs, ca, cg = coef

    def stencil(block, j, level, above, v, east, west):
        at = pl.multiple_of(block * BLOCK + j * ROWS, 8)
        cols = outer_columns(merged, block, j)
        edge = block * 8 + j
        lo = jnp.broadcast_to(south[pl.ds(edge, 1), :], (ROWS, LANES))
        hi = jnp.broadcast_to(north[pl.ds(edge, 1), :], (ROWS, LANES))
        east = jnp.where(last_lane, cols, east)
        west = jnp.where(first_lane, cols, west)
        up = jnp.where(last_row, hi, pltpu.roll(v, ROWS - 1, 0))
        dn = jnp.where(first_row, lo, pltpu.roll(v, 1, 0))
        new = level[0] * v + level[1] * east + level[2] * west + level[3] * up + level[4] * dn + level[5] * above
        field[pl.ds(at, ROWS), :] = new
        return new

    def down(block, j, level, above):
        v = field[pl.ds(pl.multiple_of(block * BLOCK + j * ROWS, 8), ROWS), :]
        return stencil(block, j, level, above, v, pltpu.roll(v, LANES - 1, 1), pltpu.roll(v, 1, 1))

    def at_level(k, refs):
        rows = pl.ds(pl.multiple_of(k * ROWS, ROWS), ROWS)
        return [ref[rows, :] for ref in refs]

    if which is not None:

        count = len(which)
        source = lax.broadcasted_iota(jnp.int32, (2 * LANES, 2 * LANES), 0) % LANES
        target = lax.broadcasted_iota(jnp.int32, (2 * LANES, 2 * LANES), 1)
        shift = jnp.where(target < LANES, target + 1, target - LANES - 1)
        shift = jnp.where(source == shift, 1.0, 0.0).astype(BF16)

        def down_body(i, carry):
            values, sides = [], []
            for u in range(UNROLL):
                k = i * UNROLL + u
                v = field[pl.ds(pl.multiple_of(k * BLOCK + which[0] * ROWS, 8), count * ROWS), :]
                high = v.astype(BF16)
                low = (v - high.astype(F32)).astype(BF16)
                values.append(v)
                sides.append(jnp.dot(jnp.concatenate([high, low], axis=1), shift, preferred_element_type=F32))
            for u in range(UNROLL):
                k = i * UNROLL + u
                level = at_level(k, (c0, ce, cw, cn, cs, ca))
                new = []
                for n, t in enumerate(which):
                    rows = slice(n * ROWS, (n + 1) * ROWS)
                    new.append(stencil(
                        k, t, level, carry[n], values[u][rows], sides[u][rows, :LANES], sides[u][rows, LANES:]
                    ))
                carry = tuple(new)
            return carry

        zero = jnp.zeros((ROWS, LANES), F32)
        last = lax.fori_loop(0, levels // UNROLL, down_body, (zero,) * count)

        def up_body(i, carry):
            k = levels - 2 - i
            g = at_level(k, (cg,))[0]
            out = []
            for t, below in zip(which, carry):
                rows = pl.ds(pl.multiple_of(k * BLOCK + t * ROWS, 8), ROWS)
                new = field[rows, :] + g * below
                field[rows, :] = new
                out.append(new)
            return tuple(out)

        lax.fori_loop(0, levels - 1, up_body, last, unroll=4)
    else:

        def down_one(a, carry):
            for b in range(8):
                carry = down(a, b, at_level(a * 8 + b, (c0, ce, cw, cn, cs, ca)), carry)
            return carry

        last = lax.fori_loop(0, levels // 8, down_one, jnp.zeros((ROWS, LANES), F32))

        def up_one(i, carry):
            for b in range(8):
                k = levels - 1 - (i * 8 + b)
                rows = pl.ds(pl.multiple_of(k * ROWS, ROWS), ROWS)
                carry = field[rows, :] + cg[rows, :] * carry
                field[rows, :] = carry
            return carry

        lax.fori_loop(0, levels // 8, up_one, jnp.zeros((ROWS, LANES), F32))


def window_kernel(
    n_lon, n_lat, levels,
    conc_hbm, adj_hbm, we_hbm, wn_hbm, mix_hbm, col_hbm, kern_hbm, obs_hbm, err_hbm,
    adj_out, force_out, res_out,
    field, conc, we, wn, mix, prof, force, c0, ce, cw, cn, cs, ca, cg,
    kv, colv, obsv, errv, sendb, recvb, kn, coln, wres, resb,
    prof2, total,
    q_adj0, q_adj1, q_one, lat_a, lat_b, lat_one_a, lat_one_b,
    w_adj0, e_adj0, w_adj1, e_adj1, s_adj0, n_adj0, s_adj1, n_adj1,
    w_one, e_one, s_one, n_one, m_adj, m_one,
    load_sem, out_sem, a2a_send, a2a_recv, res_send, res_recv, self_sem, halo_send, halo_recv, stage_sem,
):
    lon, lat = lax.axis_index("lon"), lax.axis_index("lat")
    bricks = n_lon * n_lat
    me = lon * n_lat + lat
    per = levels // 4 + 1
    tiles = bricks // 4
    groups = tiles // 8

    loads = [
        (kern_hbm, kv), (col_hbm, colv), (obs_hbm, obsv), (err_hbm, errv), (we_hbm, we), (wn_hbm, wn),
        (adj_hbm, field), (mix_hbm, mix), (conc_hbm, conc),
    ]
    loads = [pltpu.make_async_copy(a, b, load_sem.at[i]) for i, (a, b) in enumerate(loads)]
    for copy in loads:
        copy.start()

    barrier = pltpu.get_barrier_semaphore()
    for d in range(1, n_lat):
        pl.semaphore_signal(barrier, inc=1, device_id=(lon, lax.rem(lat + d, n_lat)), device_id_type=MESH)
    for d in range(1, n_lon):
        pl.semaphore_signal(barrier, inc=1, device_id=(lax.rem(lon + d, n_lon), lat), device_id_type=MESH)

    lane8 = lane_ids(8)
    for i in range(4):
        loads[i].wait()

    def pack_rows(kk, c, v):
        y = swap_blocks(v, lane8)
        for m in range(4):
            sendb[pl.ds((c * 32 + m) * per + kk, 8, stride=4 * per), :] = y[m]

    def pack_body(kk, carry):
        for c in range(groups):
            pack_rows(kk, c, [kv[pl.ds(pl.multiple_of((kk * 4 + q) * tiles + c * 8, 8), 8), :] for q in range(4)])
        return carry

    lax.fori_loop(0, levels // 4, pack_body, 0, unroll=3)
    for c in range(groups):
        rows = pl.ds(c * 8, 8)
        e = errv[rows, :]
        pack_rows(levels // 4, c, [colv[rows, :].astype(F32), obsv[rows, :], e, e])

    loads[4].wait()
    loads[5].wait()
    pack_lon(we, levels // 8, q_one.at[0])
    pack_lat(wn, levels // 8, ROWS - 1, lat_one_a.at[0])
    loads[6].wait()
    pack_lon(field, levels, q_adj0)
    pack_lat(field, levels, ROWS - 1, lat_a.at[0])
    pack_lat(field, levels, 0, lat_b.at[0])

    pl.semaphore_wait(barrier, n_lon + n_lat - 2)
    for d in range(1, n_lat):
        pl.semaphore_signal(stage_sem, inc=1, device_id=(lon, lax.rem(lat + d, n_lat)), device_id_type=MESH)
    pl.semaphore_wait(stage_sem, n_lat - 1)

    east = (lax.rem(lon + 1, n_lon), lat)
    west = (lax.rem(lon + n_lon - 1, n_lon), lat)
    north = (lon, lax.rem(lat + 1, n_lat))
    south = (lon, lax.rem(lat + n_lat - 1, n_lat))

    def remote(src, dst, index, device):
        return pltpu.make_async_remote_copy(
            src, dst, halo_send.at[index], halo_recv.at[index], device_id=device, device_id_type=MESH
        )

    def exchange(first, q, top, bottom, w, e, s, n):
        copies = [
            remote(top, s, first, north), remote(bottom, n, first + 1, south),
            remote(q, w, first + 2, east), remote(q, e, first + 3, west),
        ]
        for copy in copies:
            copy.start()
        return copies

    def land(copies):
        for copy in copies:
            copy.wait()

    wind_copies = [
        remote(q_one.at[0], w_one.at[0], 0, east), remote(lat_one_a.at[0], s_one.at[0], 1, north),
    ]
    for copy in wind_copies:
        copy.start()
    halo = exchange(2, q_adj0, lat_a.at[0], lat_b.at[0], w_adj0, e_adj0, s_adj0, n_adj0)

    lons = [lax.rem(lon + d, n_lon) for d in range(n_lon)]
    lats = [lax.rem(lat + d, n_lat) for d in range(n_lat)]
    peers = []
    for i in range(1, bricks):
        d = (i * 37) % bricks
        tl, ta = lons[d // n_lat], lats[d % n_lat]
        peers.append((tl, ta, tl * n_lat + ta))

    for tl, ta, t in peers:
        pltpu.make_async_remote_copy(
            sendb.at[pl.ds(t * per, per)], recvb.at[pl.ds(me * per, per)], a2a_send, a2a_recv,
            device_id=(tl, ta), device_id_type=MESH,
        ).start()
    own = pltpu.make_async_copy(sendb.at[pl.ds(me * per, per)], recvb.at[pl.ds(me * per, per)], self_sem)
    own.start()

    loads[7].wait()
    loads[8].wait()

    def tracer_sum(k, c):
        total = conc[pl.ds(pl.multiple_of(k * BLOCK, 8), ROWS), :]
        for t in range(1, TRACERS):
            total = total + conc[pl.ds(pl.multiple_of(k * BLOCK + t * ROWS, 8), ROWS), :]
        prof[pl.ds(pl.multiple_of(k * ROWS, 8), ROWS), :] = total
        return c

    lax.fori_loop(0, levels, tracer_sum, 0, unroll=2)

    land(wind_copies)
    lane = lane_ids(ROWS)
    row = row_ids(ROWS)
    merge_lon(w_one.at[0], w_one.at[0], (levels // 8 + 3) // 4, m_one)
    southmost = lat == 0
    northmost = lat == n_lat - 1
    open_north = jnp.logical_not(jnp.logical_and(row == ROWS - 1, northmost)).astype(F32)
    open_south = jnp.where(southmost, 0.0, 1.0)

    def coefficients(a, carry):
        above, factor = carry
        for b in range(8):
            k = a * 8 + b
            rows = pl.ds(pl.multiple_of(k * ROWS, ROWS), ROWS)
            u, n = we[rows, :], wn[rows, :]
            cols = outer_columns(m_one, a, b)
            u_west = jnp.where(lane == 0, cols, pltpu.roll(u, 1, 1))
            edge = jnp.broadcast_to(s_one[0, pl.ds(k, 1), :], (ROWS, LANES)) * open_south
            n_south = jnp.where(row == 0, edge, pltpu.roll(n, 1, 0))
            ep, wm = jnp.maximum(u, 0.0), jnp.minimum(u_west, 0.0)
            up, sm = jnp.maximum(n, 0.0), jnp.minimum(n_south, 0.0)
            below = mix[rows, :] * jnp.where(k < levels - 1, 1.0, 0.0)
            inv = 1.0 / (1.0 + below + above - above * factor)
            c0[rows, :] = (1.0 - ep + wm - up + sm) * inv
            ce[rows, :] = ep * inv
            cw[rows, :] = -wm * inv
            cn[rows, :] = up * open_north * inv
            cs[rows, :] = -sm * inv
            ca[rows, :] = above * inv
            factor = below * inv
            cg[rows, :] = factor
            above = below
        return above, factor

    zero = jnp.zeros((ROWS, LANES), F32)
    lax.fori_loop(0, levels // 8, coefficients, (zero, zero))
    coef = (c0, ce, cw, cn, cs, ca, cg)

    land(halo)
    merge_lon(w_adj0, e_adj0, levels // 4, m_adj)
    transport(field, levels, range(TRACERS), m_adj, s_adj0, n_adj0, coef)
    pack_lon(field, levels, q_adj1)
    pack_lat(field, levels, ROWS - 1, lat_a.at[1])
    pack_lat(field, levels, 0, lat_b.at[1])
    adj_halo = exchange(6, q_adj1, lat_a.at[1], lat_b.at[1], w_adj1, e_adj1, s_adj1, n_adj1)

    own.wait()
    rest = pl.ds(0, (bricks - 1) * per)
    pltpu.make_async_copy(recvb.at[rest], recvb.at[rest], a2a_recv).wait()

    def unpack(kk, c):
        z = [recvb[pl.ds((c * 32 + m) * per + kk, 8, stride=4 * per), :] for m in range(4)]
        return swap_blocks(z, lane8)

    def unpack_body(kk, carry):
        for c in range(groups):
            v = unpack(kk, c)
            for q in range(4):
                kn[pl.ds(pl.multiple_of((kk * 4 + q) * tiles + c * 8, 8), 8), :] = v[q]
        return carry

    lax.fori_loop(0, levels // 4, unpack_body, 0, unroll=3)
    for c in range(groups):
        rows = pl.ds(c * 8, 8)
        aux = unpack(levels // 4, c)
        coln[rows, :] = aux[0].astype(jnp.int32)
        obsv[rows, :] = aux[1]
        errv[rows, :] = aux[2]

    for r in range(ROWS):
        v = prof[pl.ds(r, levels, stride=ROWS), :]
        high = v.astype(BF16)
        rows, at = pl.ds(r // 2 * levels, levels), r % 2 * LANES
        prof2[rows, pl.ds(at, LANES)] = high
        prof2[rows, pl.ds(2 * LANES + at, LANES)] = (v - high.astype(F32)).astype(BF16)

    cell = lax.broadcasted_iota(jnp.int32, (2 * LANES, 2 * LANES), 0)

    def pair_of(ref, i):
        return jnp.concatenate([ref[pl.ds(2 * i, 1), :], ref[pl.ds(2 * i + 1, 1), :]], axis=1)

    def soundings(i, carry):
        col, obs, err = pair_of(coln, i), pair_of(obsv, i), pair_of(errv, i)
        half = lax.shift_right_arithmetic(col, 8)
        hot = jnp.where(lax.bitwise_and(col, 2 * LANES - 1) == cell, 1.0, 0.0).astype(BF16)
        g = jnp.dot(prof2[...], jnp.concatenate([hot, hot], axis=0), preferred_element_type=F32)
        parts = [g[r * levels : (r + 1) * levels] for r in range(ROWS // 2)]
        for b in range(3):
            bit = lax.bitwise_and(half, 1 << b) != 0
            parts = [jnp.where(bit, parts[2 * j + 1], parts[2 * j]) for j in range(len(parts) // 2)]
        w = jnp.concatenate(
            [kn[pl.ds(2 * i, levels, stride=tiles), :], kn[pl.ds(2 * i + 1, levels, stride=tiles), :]], axis=1
        )
        modelled = jnp.sum(w * parts[0], axis=0, keepdims=True)
        res = jnp.where(col >= 0, (modelled - obs) / err, 0.0)
        wres[pl.ds(2 * i, 1), :] = res[:, :LANES]
        wres[pl.ds(2 * i + 1, 1), :] = res[:, LANES:]
        w = w * (res / err)
        high = w.astype(BF16).astype(F32)
        low = w - high
        lhs = jnp.concatenate(
            [jnp.where(half == r, v, 0.0) for v in (high, low) for r in range(ROWS // 2)], axis=0
        ).astype(BF16)
        total[...] += lax.dot_general(lhs, hot, (((1,), (1,)), ((), ())), preferred_element_type=F32)
        return carry

    total[...] = jnp.zeros_like(total)
    lax.fori_loop(0, tiles // 2, soundings, 0, unroll=4)

    for r in range(ROWS):
        lanes = pl.ds(r % 2 * LANES, LANES)
        at = r // 2 * levels
        force[pl.ds(r, levels, stride=ROWS), :] = (
            total[pl.ds(at, levels), lanes] + total[pl.ds(levels * ROWS // 2 + at, levels), lanes]
        )

    def send_force(step):
        pack_lon(force, levels // 8, q_one.at[step])
        pack_lat(force, levels // 8, ROWS - 1, lat_one_a.at[step])
        pack_lat(force, levels // 8, 0, lat_one_b.at[step])
        return exchange(
            6 + 4 * step, q_one.at[step], lat_one_a.at[step], lat_one_b.at[step],
            w_one.at[step], e_one.at[step], s_one.at[step], n_one.at[step],
        )

    def step_force(step, halo):
        land(halo)
        merge_lon(w_one.at[step], e_one.at[step], (levels // 8 + 3) // 4, m_one)
        transport(force, levels, None, m_one, s_one.at[step], n_one.at[step], coef)

    halo = send_force(1)
    land(adj_halo)
    merge_lon(w_adj1, e_adj1, levels // 4, m_adj)
    transport(field, levels, range(0, TRACERS // 2), m_adj, s_adj1, n_adj1, coef)
    step_force(1, halo)
    halo = send_force(2)
    for tl, ta, t in peers:
        pltpu.make_async_remote_copy(
            wres.at[pl.ds(t // 4, 1)], resb.at[pl.ds(me, 1)], res_send, res_recv,
            device_id=(tl, ta), device_id_type=MESH,
        ).start()
    own_res = pltpu.make_async_copy(wres.at[pl.ds(me // 4, 1)], resb.at[pl.ds(me, 1)], self_sem)
    own_res.start()

    transport(field, levels, range(TRACERS // 2, TRACERS), m_adj, s_adj1, n_adj1, coef)
    adj_copy = pltpu.make_async_copy(field, adj_out, out_sem.at[0])
    adj_copy.start()
    step_force(2, halo)
    force_copy = pltpu.make_async_copy(force, force_out, out_sem.at[1])
    force_copy.start()

    own_res.wait()
    rest_res = pl.ds(0, bricks - 1)
    pltpu.make_async_copy(resb.at[rest_res], resb.at[rest_res], res_recv).wait()
    mine_block = lax.rem(me, 4)
    for g in range(groups):
        mine = jnp.zeros((8, LANES), F32)
        for m in range(4):
            v = resb[pl.ds(g * 32 + m, 8, stride=4), :]
            shift = lax.rem((m - mine_block + 4) * 32, LANES)
            mine = jnp.where(lane8 // 32 == m, pltpu.roll(v, shift, 1), mine)
        errv[pl.ds(g * 8, 8), :] = mine
    res_copy = pltpu.make_async_copy(errv, res_out, out_sem.at[2])
    res_copy.start()

    pltpu.make_async_copy(recvb.at[rest], recvb.at[rest], a2a_send).wait()
    pltpu.make_async_copy(resb.at[rest_res], resb.at[rest_res], res_send).wait()
    adj_copy.wait()
    force_copy.wait()
    res_copy.wait()


def add_kernel(levels, field, force, res, out, res_out, buf, one, rows_buf, in_sem, out_sem, aux_sem):
    parts = levels // COMBINE
    rows = COMBINE * BLOCK
    aux = [
        pltpu.make_async_copy(force, one, aux_sem.at[0]), pltpu.make_async_copy(res, rows_buf, aux_sem.at[1]),
        pltpu.make_async_copy(rows_buf, res_out, aux_sem.at[2]),
    ]
    aux[0].start()
    reads, writes = [], []
    for p in range(parts):
        at = pl.ds(p * rows, rows)
        reads.append(pltpu.make_async_copy(field.at[at], buf.at[at], in_sem.at[p]))
        writes.append(pltpu.make_async_copy(buf.at[at], out.at[at], out_sem.at[p]))
        reads[p].start()
    aux[1].start()
    aux[0].wait()
    for p in range(parts):
        reads[p].wait()

        def body(k, c):
            add = one[pl.ds(pl.multiple_of(k * ROWS, ROWS), ROWS), :]
            for t in range(TRACERS):
                at = pl.ds(pl.multiple_of(k * BLOCK + t * ROWS, ROWS), ROWS)
                buf[at, :] = buf[at, :] + add
            return c

        lax.fori_loop(p * COMBINE, (p + 1) * COMBINE, body, 0, unroll=4)
        writes[p].start()
        if p == 0:
            aux[1].wait()
            aux[2].start()
    for copy in writes:
        copy.wait()
    aux[2].wait()


def per_device(n_lon, n_lat, concentration, adjoint, wind_east, wind_north, mixing, sound_col, kernel, observed, obs_error):
    levels, tracers, row_count, col_count = adjoint.shape
    bricks = n_lon * n_lat
    slots = sound_col.shape[2]
    tiles = slots // LANES
    per = levels // 4 + 1
    big, one = (levels * BLOCK, LANES), (levels * ROWS, LANES)
    q_rows, q_one_rows = levels // 4 * 8, (levels // 8 + 3) // 4 * 8
    hbm = pl.BlockSpec(memory_space=pl.ANY)
    vm = lambda *shape: pltpu.VMEM(shape, F32)
    scratch = (
        [vm(*big), vm(*big)] + [vm(*one)] * 12
        + [vm(levels * tiles, LANES), pltpu.VMEM((tiles, LANES), jnp.int32), vm(tiles, LANES), vm(tiles, LANES)]
        + [vm(bricks * per, LANES), vm(bricks * per, LANES), vm(levels * tiles, LANES)]
        + [pltpu.VMEM((tiles, LANES), jnp.int32), vm(tiles, LANES), vm(bricks, LANES)]
        + [pltpu.VMEM((ROWS // 2 * levels, 4 * LANES), BF16), vm(ROWS * levels, 2 * LANES)]
        + [vm(q_rows, LANES), vm(q_rows, LANES), vm(3, q_one_rows, LANES)]
        + [vm(2, levels * 8, LANES), vm(2, levels * 8, LANES), vm(3, levels, LANES), vm(3, levels, LANES)]
        + [vm(q_rows, LANES)] * 4 + [vm(levels * 8, LANES)] * 4
        + [vm(3, q_one_rows, LANES), vm(3, q_one_rows, LANES), vm(3, levels, LANES), vm(3, levels, LANES)]
        + [vm(q_rows, LANES), vm(q_one_rows, LANES)]
        + [pltpu.SemaphoreType.DMA((9,)), pltpu.SemaphoreType.DMA((3,))]
        + [pltpu.SemaphoreType.DMA] * 5
        + [pltpu.SemaphoreType.DMA((18,)), pltpu.SemaphoreType.DMA((18,)), pltpu.SemaphoreType.REGULAR]
    )
    field, force, res = pl.pallas_call(
        functools.partial(window_kernel, n_lon, n_lat, levels),
        out_shape=(
            jax.ShapeDtypeStruct(big, F32), jax.ShapeDtypeStruct(one, F32), jax.ShapeDtypeStruct((tiles, LANES), F32),
        ),
        in_specs=[hbm] * 9,
        out_specs=(hbm,) * 3,
        scratch_shapes=scratch,
        compiler_params=pltpu.CompilerParams(collective_id=0, has_side_effects=True, vmem_limit_bytes=62 << 20),
        name="window",
    )(
        concentration.reshape(big), adjoint.reshape(big), wind_east.reshape(one), wind_north.reshape(one),
        mixing.reshape(one), sound_col.reshape(tiles, LANES), kernel.reshape(levels * tiles, LANES),
        observed.reshape(tiles, LANES), obs_error.reshape(tiles, LANES),
    )
    parts = levels // COMBINE
    out, residual = pl.pallas_call(
        functools.partial(add_kernel, levels),
        out_shape=(jax.ShapeDtypeStruct(big, F32), jax.ShapeDtypeStruct((tiles, LANES), F32)),
        in_specs=[hbm] * 3,
        out_specs=(hbm, hbm),
        scratch_shapes=[
            vm(*big), vm(*one), vm(tiles, LANES),
            pltpu.SemaphoreType.DMA((parts,)), pltpu.SemaphoreType.DMA((parts,)), pltpu.SemaphoreType.DMA((3,)),
        ],
        compiler_params=pltpu.CompilerParams(vmem_limit_bytes=62 << 20),
        name="combine",
    )(field, force, res)
    return out.reshape(adjoint.shape), residual.reshape(observed.shape)


def solution(mesh):
    in_specs = (
        P(None, None, "lat", "lon"),
        P(None, None, "lat", "lon"),
        P(None, "lat", "lon"),
        P(None, "lat", "lon"),
        P(None, "lat", "lon"),
        P(None, ("lon", "lat"), None),
        P(None, ("lon", "lat"), None),
        P(None, ("lon", "lat"), None),
        P(None, ("lon", "lat"), None),
    )
    out_specs = (P(None, None, "lat", "lon"), P(None, ("lon", "lat"), None))
    return jax.shard_map(
        functools.partial(per_device, mesh.shape["lon"], mesh.shape["lat"]),
        mesh=mesh, in_specs=in_specs, out_specs=out_specs, check_vma=False,
    )
```

```python
import functools

import jax
import jax.numpy as jnp
from jax import lax
from jax.experimental import pallas as pl
from jax.experimental.pallas import tpu as pltpu
from jax.sharding import PartitionSpec as P

MESH = pl.DeviceIdType.MESH
LANES = 128
ROWS = 16
TRACERS = 8
BLOCK = TRACERS * ROWS
COMBINE = 8
UNROLL = 8
F32 = jnp.float32
BF16 = jnp.bfloat16


def lane_ids(rows):
    return lax.broadcasted_iota(jnp.int32, (rows, LANES), 1)


def row_ids(rows):
    return lax.broadcasted_iota(jnp.int32, (rows, LANES), 0)


def swap_blocks(v, lane):
    low = lane < 64
    even = (lane // 32) % 2 == 0
    out = []
    first = [None] * 4
    for b in range(2):
        first[b] = jnp.where(low, v[b], pltpu.roll(v[2 + b], 64, 1))
        first[2 + b] = jnp.where(low, pltpu.roll(v[b], 64, 1), v[2 + b])
    for h in range(2):
        a, b = first[2 * h], first[2 * h + 1]
        out.append(jnp.where(even, a, pltpu.roll(b, 32, 1)))
        out.append(jnp.where(even, pltpu.roll(a, 96, 1), b))
    return out


def pack_lon(src, blocks, dst):
    pair = ((lane_ids(8) + 127) % 128) // 2
    bits = [lax.bitwise_and(pair, 1 << b) != 0 for b in range(6)]

    def tree(parts, level):
        while len(parts) > 1:
            parts = [jnp.where(bits[level], parts[2 * i + 1], parts[2 * i]) for i in range(len(parts) // 2)]
            level += 1
        return parts[0]

    def group(g, count):
        blocks_out = []
        for kk in range(count):
            parts = []
            for j in range(16):
                v = src[pl.ds(pl.multiple_of((g * 4 + kk) * BLOCK + j * 8, 8), 8), :]
                parts.append(pltpu.roll(v, (2 * (kk * 16 + j) + 2) % LANES, 1))
            blocks_out.append(tree(parts, 0))
        blocks_out = (blocks_out * 4)[:4] if count < 4 else blocks_out
        dst[pl.ds(pl.multiple_of(g * 8, 8), 8), :] = tree(blocks_out, 4)

    def body(g, c):
        group(g, 4)
        return c

    lax.fori_loop(0, blocks // 4, body, 0, unroll=3)
    if blocks % 4:
        group(blocks // 4, blocks % 4)


def pack_lat(src, blocks, row, dst):
    def body(k, c):
        dst[pl.ds(pl.multiple_of(k * 8, 8), 8), :] = src[pl.ds(k * BLOCK + row, 8, stride=ROWS), :]
        return c

    lax.fori_loop(0, blocks, body, 0, unroll=3)


def merge_lon(west, east, groups, dst):
    odd = lane_ids(8) % 2 == 1

    def body(g, c):
        rows = pl.ds(pl.multiple_of(g * 8, 8), 8)
        dst[rows, :] = jnp.where(odd, west[rows, :], pltpu.roll(east[rows, :], 126, 1))
        return c

    lax.fori_loop(0, groups, body, 0)


def outer_columns(merged, block, j):
    rows = pl.ds(pl.multiple_of((block // 4) * 8, 8), 8)
    v = merged[rows, :]
    slot = lax.rem(block, 4) * 16 + 2 * j
    return jnp.concatenate(
        [pltpu.roll(v, LANES - 1 - 2 * slot, 1), pltpu.roll(v, LANES - 3 - 2 * slot, 1)], axis=0
    )


def transport(field, levels, which, merged, south, north, coef):
    lane = lane_ids(ROWS)
    row = row_ids(ROWS)
    first_lane, last_lane = lane == 0, lane == LANES - 1
    first_row, last_row = row == 0, row == ROWS - 1
    c0, ce, cw, cn, cs, ca, cg = coef

    def stencil(block, j, level, above, v, east, west):
        at = pl.multiple_of(block * BLOCK + j * ROWS, 8)
        cols = outer_columns(merged, block, j)
        edge = block * 8 + j
        lo = jnp.broadcast_to(south[pl.ds(edge, 1), :], (ROWS, LANES))
        hi = jnp.broadcast_to(north[pl.ds(edge, 1), :], (ROWS, LANES))
        east = jnp.where(last_lane, cols, east)
        west = jnp.where(first_lane, cols, west)
        up = jnp.where(last_row, hi, pltpu.roll(v, ROWS - 1, 0))
        dn = jnp.where(first_row, lo, pltpu.roll(v, 1, 0))
        new = level[0] * v + level[1] * east + level[2] * west + level[3] * up + level[4] * dn + level[5] * above
        field[pl.ds(at, ROWS), :] = new
        return new

    def down(block, j, level, above):
        v = field[pl.ds(pl.multiple_of(block * BLOCK + j * ROWS, 8), ROWS), :]
        return stencil(block, j, level, above, v, pltpu.roll(v, LANES - 1, 1), pltpu.roll(v, 1, 1))

    def at_level(k, refs):
        rows = pl.ds(pl.multiple_of(k * ROWS, ROWS), ROWS)
        return [ref[rows, :] for ref in refs]

    if which is not None:

        count = len(which)
        source = lax.broadcasted_iota(jnp.int32, (2 * LANES, 2 * LANES), 0) % LANES
        target = lax.broadcasted_iota(jnp.int32, (2 * LANES, 2 * LANES), 1)
        shift = jnp.where(target < LANES, target + 1, target - LANES - 1)
        shift = jnp.where(source == shift, 1.0, 0.0).astype(BF16)

        def down_body(i, carry):
            values, sides = [], []
            for u in range(UNROLL):
                k = i * UNROLL + u
                v = field[pl.ds(pl.multiple_of(k * BLOCK + which[0] * ROWS, 8), count * ROWS), :]
                high = v.astype(BF16)
                low = (v - high.astype(F32)).astype(BF16)
                values.append(v)
                sides.append(jnp.dot(jnp.concatenate([high, low], axis=1), shift, preferred_element_type=F32))
            for u in range(UNROLL):
                k = i * UNROLL + u
                level = at_level(k, (c0, ce, cw, cn, cs, ca))
                new = []
                for n, t in enumerate(which):
                    rows = slice(n * ROWS, (n + 1) * ROWS)
                    new.append(stencil(
                        k, t, level, carry[n], values[u][rows], sides[u][rows, :LANES], sides[u][rows, LANES:]
                    ))
                carry = tuple(new)
            return carry

        zero = jnp.zeros((ROWS, LANES), F32)
        last = lax.fori_loop(0, levels // UNROLL, down_body, (zero,) * count)

        def up_body(i, carry):
            k = levels - 2 - i
            g = at_level(k, (cg,))[0]
            out = []
            for t, below in zip(which, carry):
                rows = pl.ds(pl.multiple_of(k * BLOCK + t * ROWS, 8), ROWS)
                new = field[rows, :] + g * below
                field[rows, :] = new
                out.append(new)
            return tuple(out)

        lax.fori_loop(0, levels - 1, up_body, last, unroll=4)
    else:

        def down_one(a, carry):
            for b in range(8):
                carry = down(a, b, at_level(a * 8 + b, (c0, ce, cw, cn, cs, ca)), carry)
            return carry

        last = lax.fori_loop(0, levels // 8, down_one, jnp.zeros((ROWS, LANES), F32))

        def up_one(i, carry):
            for b in range(8):
                k = levels - 1 - (i * 8 + b)
                rows = pl.ds(pl.multiple_of(k * ROWS, ROWS), ROWS)
                carry = field[rows, :] + cg[rows, :] * carry
                field[rows, :] = carry
            return carry

        lax.fori_loop(0, levels // 8, up_one, jnp.zeros((ROWS, LANES), F32))


def window_kernel(
    n_lon, n_lat, levels,
    conc_hbm, adj_hbm, we_hbm, wn_hbm, mix_hbm, col_hbm, kern_hbm, obs_hbm, err_hbm,
    adj_out, force_out, res_out,
    field, conc, we, wn, mix, prof, force, c0, ce, cw, cn, cs, ca, cg,
    kv, colv, obsv, errv, sendb, recvb, kn, coln, wres, resb,
    prof2, total,
    q_adj0, q_adj1, q_one, lat_a, lat_b, lat_one_a, lat_one_b,
    w_adj0, e_adj0, w_adj1, e_adj1, s_adj0, n_adj0, s_adj1, n_adj1,
    w_one, e_one, s_one, n_one, m_adj, m_one,
    load_sem, out_sem, a2a_send, a2a_recv, res_send, res_recv, self_sem, halo_send, halo_recv, stage_sem,
):
    lon, lat = lax.axis_index("lon"), lax.axis_index("lat")
    bricks = n_lon * n_lat
    me = lon * n_lat + lat
    per = levels // 4 + 1
    tiles = bricks // 4
    groups = tiles // 8

    loads = [
        (kern_hbm, kv), (col_hbm, colv), (obs_hbm, obsv), (err_hbm, errv), (we_hbm, we), (wn_hbm, wn),
        (adj_hbm, field), (mix_hbm, mix), (conc_hbm, conc),
    ]
    loads = [pltpu.make_async_copy(a, b, load_sem.at[i]) for i, (a, b) in enumerate(loads)]
    for copy in loads:
        copy.start()

    barrier = pltpu.get_barrier_semaphore()
    for d in range(1, n_lat):
        pl.semaphore_signal(barrier, inc=1, device_id=(lon, lax.rem(lat + d, n_lat)), device_id_type=MESH)
    for d in range(1, n_lon):
        pl.semaphore_signal(barrier, inc=1, device_id=(lax.rem(lon + d, n_lon), lat), device_id_type=MESH)

    lane8 = lane_ids(8)

    def pack_soundings():
        for i in range(4):
            loads[i].wait()

        def pack_rows(kk, c, v):
            y = swap_blocks(v, lane8)
            for m in range(4):
                sendb[pl.ds((c * 32 + m) * per + kk, 8, stride=4 * per), :] = y[m]

        def pack_body(kk, carry):
            for c in range(groups):
                pack_rows(kk, c, [kv[pl.ds(pl.multiple_of((kk * 4 + q) * tiles + c * 8, 8), 8), :] for q in range(4)])
            return carry

        lax.fori_loop(0, levels // 4, pack_body, 0, unroll=3)
        for c in range(groups):
            rows = pl.ds(c * 8, 8)
            e = errv[rows, :]
            pack_rows(levels // 4, c, [colv[rows, :].astype(F32), obsv[rows, :], e, e])


    def pack_halos():
        loads[4].wait()
        loads[5].wait()
        pack_lon(we, levels // 8, q_one.at[0])
        pack_lat(wn, levels // 8, ROWS - 1, lat_one_a.at[0])
        loads[6].wait()
        pack_lon(field, levels, q_adj0)
        pack_lat(field, levels, ROWS - 1, lat_a.at[0])
        pack_lat(field, levels, 0, lat_b.at[0])


    def enter():
        pl.semaphore_wait(barrier, n_lon + n_lat - 2)
        for d in range(1, n_lat):
            pl.semaphore_signal(stage_sem, inc=1, device_id=(lon, lax.rem(lat + d, n_lat)), device_id_type=MESH)
        pl.semaphore_wait(stage_sem, n_lat - 1)

    east = (lax.rem(lon + 1, n_lon), lat)
    west = (lax.rem(lon + n_lon - 1, n_lon), lat)
    north = (lon, lax.rem(lat + 1, n_lat))
    south = (lon, lax.rem(lat + n_lat - 1, n_lat))

    def remote(src, dst, index, device):
        return pltpu.make_async_remote_copy(
            src, dst, halo_send.at[index], halo_recv.at[index], device_id=device, device_id_type=MESH
        )

    def exchange(first, q, top, bottom, w, e, s, n):
        copies = [
            remote(top, s, first, north), remote(bottom, n, first + 1, south),
            remote(q, w, first + 2, east), remote(q, e, first + 3, west),
        ]
        for copy in copies:
            copy.start()
        return copies

    def land(copies):
        for copy in copies:
            copy.wait()

    def send_halos():
        wind_copies = [
            remote(q_one.at[0], w_one.at[0], 0, east), remote(lat_one_a.at[0], s_one.at[0], 1, north),
        ]
        for copy in wind_copies:
            copy.start()
        halo = exchange(2, q_adj0, lat_a.at[0], lat_b.at[0], w_adj0, e_adj0, s_adj0, n_adj0)
        return wind_copies, halo

    lons = [lax.rem(lon + d, n_lon) for d in range(n_lon)]
    lats = [lax.rem(lat + d, n_lat) for d in range(n_lat)]
    peers = []
    for i in range(1, bricks):
        d = (i * 37) % bricks
        tl, ta = lons[d // n_lat], lats[d % n_lat]
        peers.append((tl, ta, tl * n_lat + ta))

    def send_soundings(which):
        for tl, ta, t in which:
            pltpu.make_async_remote_copy(
                sendb.at[pl.ds(t * per, per)], recvb.at[pl.ds(me * per, per)], a2a_send, a2a_recv,
                device_id=(tl, ta), device_id_type=MESH,
            ).start()

    def sum_tracers():
        loads[8].wait()

        def tracer_sum(k, c):
            total = conc[pl.ds(pl.multiple_of(k * BLOCK, 8), ROWS), :]
            for t in range(1, TRACERS):
                total = total + conc[pl.ds(pl.multiple_of(k * BLOCK + t * ROWS, 8), ROWS), :]
            prof[pl.ds(pl.multiple_of(k * ROWS, 8), ROWS), :] = total
            return c

        lax.fori_loop(0, levels, tracer_sum, 0, unroll=2)

    own = pltpu.make_async_copy(sendb.at[pl.ds(me * per, per)], recvb.at[pl.ds(me * per, per)], self_sem)
    pack_soundings()
    enter()
    send_soundings(peers[: bricks // 2])
    pack_halos()
    wind_copies, halo = send_halos()
    send_soundings(peers[bricks // 2 :])
    own.start()
    sum_tracers()
    loads[7].wait()

    land(wind_copies)
    lane = lane_ids(ROWS)
    row = row_ids(ROWS)
    merge_lon(w_one.at[0], w_one.at[0], (levels // 8 + 3) // 4, m_one)
    southmost = lat == 0
    northmost = lat == n_lat - 1
    open_north = jnp.logical_not(jnp.logical_and(row == ROWS - 1, northmost)).astype(F32)
    open_south = jnp.where(southmost, 0.0, 1.0)

    def coefficients(a, carry):
        above, factor = carry
        for b in range(8):
            k = a * 8 + b
            rows = pl.ds(pl.multiple_of(k * ROWS, ROWS), ROWS)
            u, n = we[rows, :], wn[rows, :]
            cols = outer_columns(m_one, a, b)
            u_west = jnp.where(lane == 0, cols, pltpu.roll(u, 1, 1))
            edge = jnp.broadcast_to(s_one[0, pl.ds(k, 1), :], (ROWS, LANES)) * open_south
            n_south = jnp.where(row == 0, edge, pltpu.roll(n, 1, 0))
            ep, wm = jnp.maximum(u, 0.0), jnp.minimum(u_west, 0.0)
            up, sm = jnp.maximum(n, 0.0), jnp.minimum(n_south, 0.0)
            below = mix[rows, :] * jnp.where(k < levels - 1, 1.0, 0.0)
            inv = 1.0 / (1.0 + below + above - above * factor)
            c0[rows, :] = (1.0 - ep + wm - up + sm) * inv
            ce[rows, :] = ep * inv
            cw[rows, :] = -wm * inv
            cn[rows, :] = up * open_north * inv
            cs[rows, :] = -sm * inv
            ca[rows, :] = above * inv
            factor = below * inv
            cg[rows, :] = factor
            above = below
        return above, factor

    zero = jnp.zeros((ROWS, LANES), F32)
    lax.fori_loop(0, levels // 8, coefficients, (zero, zero))
    coef = (c0, ce, cw, cn, cs, ca, cg)

    land(halo)
    merge_lon(w_adj0, e_adj0, levels // 4, m_adj)
    transport(field, levels, range(TRACERS), m_adj, s_adj0, n_adj0, coef)
    pack_lon(field, levels, q_adj1)
    pack_lat(field, levels, ROWS - 1, lat_a.at[1])
    pack_lat(field, levels, 0, lat_b.at[1])
    adj_halo = exchange(6, q_adj1, lat_a.at[1], lat_b.at[1], w_adj1, e_adj1, s_adj1, n_adj1)

    own.wait()
    rest = pl.ds(0, (bricks - 1) * per)
    pltpu.make_async_copy(recvb.at[rest], recvb.at[rest], a2a_recv).wait()

    def unpack(kk, c):
        z = [recvb[pl.ds((c * 32 + m) * per + kk, 8, stride=4 * per), :] for m in range(4)]
        return swap_blocks(z, lane8)

    def unpack_body(kk, carry):
        for c in range(groups):
            v = unpack(kk, c)
            for q in range(4):
                kn[pl.ds(pl.multiple_of((kk * 4 + q) * tiles + c * 8, 8), 8), :] = v[q]
        return carry

    lax.fori_loop(0, levels // 4, unpack_body, 0, unroll=3)
    for c in range(groups):
        rows = pl.ds(c * 8, 8)
        aux = unpack(levels // 4, c)
        coln[rows, :] = aux[0].astype(jnp.int32)
        obsv[rows, :] = aux[1]
        errv[rows, :] = aux[2]

    for r in range(ROWS):
        v = prof[pl.ds(r, levels, stride=ROWS), :]
        high = v.astype(BF16)
        rows, at = pl.ds(r // 2 * levels, levels), r % 2 * LANES
        prof2[rows, pl.ds(at, LANES)] = high
        prof2[rows, pl.ds(2 * LANES + at, LANES)] = (v - high.astype(F32)).astype(BF16)

    cell = lax.broadcasted_iota(jnp.int32, (2 * LANES, 2 * LANES), 0)

    def pair_of(ref, i):
        return jnp.concatenate([ref[pl.ds(2 * i, 1), :], ref[pl.ds(2 * i + 1, 1), :]], axis=1)

    def soundings(i, carry):
        col, obs, err = pair_of(coln, i), pair_of(obsv, i), pair_of(errv, i)
        half = lax.shift_right_arithmetic(col, 8)
        hot = jnp.where(lax.bitwise_and(col, 2 * LANES - 1) == cell, 1.0, 0.0).astype(BF16)
        g = jnp.dot(prof2[...], jnp.concatenate([hot, hot], axis=0), preferred_element_type=F32)
        parts = [g[r * levels : (r + 1) * levels] for r in range(ROWS // 2)]
        for b in range(3):
            bit = lax.bitwise_and(half, 1 << b) != 0
            parts = [jnp.where(bit, parts[2 * j + 1], parts[2 * j]) for j in range(len(parts) // 2)]
        w = jnp.concatenate(
            [kn[pl.ds(2 * i, levels, stride=tiles), :], kn[pl.ds(2 * i + 1, levels, stride=tiles), :]], axis=1
        )
        modelled = jnp.sum(w * parts[0], axis=0, keepdims=True)
        res = jnp.where(col >= 0, (modelled - obs) / err, 0.0)
        wres[pl.ds(2 * i, 1), :] = res[:, :LANES]
        wres[pl.ds(2 * i + 1, 1), :] = res[:, LANES:]
        w = w * (res / err)
        high = w.astype(BF16).astype(F32)
        low = w - high
        lhs = jnp.concatenate(
            [jnp.where(half == r, v, 0.0) for v in (high, low) for r in range(ROWS // 2)], axis=0
        ).astype(BF16)
        total[...] += lax.dot_general(lhs, hot, (((1,), (1,)), ((), ())), preferred_element_type=F32)
        return carry

    total[...] = jnp.zeros_like(total)
    lax.fori_loop(0, tiles // 2, soundings, 0, unroll=4)

    for r in range(ROWS):
        lanes = pl.ds(r % 2 * LANES, LANES)
        at = r // 2 * levels
        force[pl.ds(r, levels, stride=ROWS), :] = (
            total[pl.ds(at, levels), lanes] + total[pl.ds(levels * ROWS // 2 + at, levels), lanes]
        )

    def send_force(step):
        pack_lon(force, levels // 8, q_one.at[step])
        pack_lat(force, levels // 8, ROWS - 1, lat_one_a.at[step])
        pack_lat(force, levels // 8, 0, lat_one_b.at[step])
        return exchange(
            6 + 4 * step, q_one.at[step], lat_one_a.at[step], lat_one_b.at[step],
            w_one.at[step], e_one.at[step], s_one.at[step], n_one.at[step],
        )

    def step_force(step, halo):
        land(halo)
        merge_lon(w_one.at[step], e_one.at[step], (levels // 8 + 3) // 4, m_one)
        transport(force, levels, None, m_one, s_one.at[step], n_one.at[step], coef)

    halo = send_force(1)
    land(adj_halo)
    merge_lon(w_adj1, e_adj1, levels // 4, m_adj)
    transport(field, levels, range(0, TRACERS // 2), m_adj, s_adj1, n_adj1, coef)
    step_force(1, halo)
    halo = send_force(2)
    for tl, ta, t in peers:
        pltpu.make_async_remote_copy(
            wres.at[pl.ds(t // 4, 1)], resb.at[pl.ds(me, 1)], res_send, res_recv,
            device_id=(tl, ta), device_id_type=MESH,
        ).start()
    own_res = pltpu.make_async_copy(wres.at[pl.ds(me // 4, 1)], resb.at[pl.ds(me, 1)], self_sem)
    own_res.start()

    transport(field, levels, range(TRACERS // 2, TRACERS), m_adj, s_adj1, n_adj1, coef)
    adj_copy = pltpu.make_async_copy(field, adj_out, out_sem.at[0])
    adj_copy.start()
    step_force(2, halo)
    force_copy = pltpu.make_async_copy(force, force_out, out_sem.at[1])
    force_copy.start()

    own_res.wait()
    rest_res = pl.ds(0, bricks - 1)
    pltpu.make_async_copy(resb.at[rest_res], resb.at[rest_res], res_recv).wait()
    mine_block = lax.rem(me, 4)
    for g in range(groups):
        mine = jnp.zeros((8, LANES), F32)
        for m in range(4):
            v = resb[pl.ds(g * 32 + m, 8, stride=4), :]
            shift = lax.rem((m - mine_block + 4) * 32, LANES)
            mine = jnp.where(lane8 // 32 == m, pltpu.roll(v, shift, 1), mine)
        errv[pl.ds(g * 8, 8), :] = mine
    res_copy = pltpu.make_async_copy(errv, res_out, out_sem.at[2])
    res_copy.start()

    pltpu.make_async_copy(recvb.at[rest], recvb.at[rest], a2a_send).wait()
    pltpu.make_async_copy(resb.at[rest_res], resb.at[rest_res], res_send).wait()
    adj_copy.wait()
    force_copy.wait()
    res_copy.wait()


def add_kernel(levels, field, force, res, out, res_out, buf, one, rows_buf, in_sem, out_sem, aux_sem):
    parts = levels // COMBINE
    rows = COMBINE * BLOCK
    aux = [
        pltpu.make_async_copy(force, one, aux_sem.at[0]), pltpu.make_async_copy(res, rows_buf, aux_sem.at[1]),
        pltpu.make_async_copy(rows_buf, res_out, aux_sem.at[2]),
    ]
    aux[0].start()
    reads, writes = [], []
    for p in range(parts):
        at = pl.ds(p * rows, rows)
        reads.append(pltpu.make_async_copy(field.at[at], buf.at[at], in_sem.at[p]))
        writes.append(pltpu.make_async_copy(buf.at[at], out.at[at], out_sem.at[p]))
        reads[p].start()
    aux[1].start()
    aux[0].wait()
    for p in range(parts):
        reads[p].wait()

        def body(k, c):
            add = one[pl.ds(pl.multiple_of(k * ROWS, ROWS), ROWS), :]
            for t in range(TRACERS):
                at = pl.ds(pl.multiple_of(k * BLOCK + t * ROWS, ROWS), ROWS)
                buf[at, :] = buf[at, :] + add
            return c

        lax.fori_loop(p * COMBINE, (p + 1) * COMBINE, body, 0, unroll=4)
        writes[p].start()
        if p == 0:
            aux[1].wait()
            aux[2].start()
    for copy in writes:
        copy.wait()
    aux[2].wait()


def per_device(n_lon, n_lat, concentration, adjoint, wind_east, wind_north, mixing, sound_col, kernel, observed, obs_error):
    levels, tracers, row_count, col_count = adjoint.shape
    bricks = n_lon * n_lat
    slots = sound_col.shape[2]
    tiles = slots // LANES
    per = levels // 4 + 1
    big, one = (levels * BLOCK, LANES), (levels * ROWS, LANES)
    q_rows, q_one_rows = levels // 4 * 8, (levels // 8 + 3) // 4 * 8
    hbm = pl.BlockSpec(memory_space=pl.ANY)
    vm = lambda *shape: pltpu.VMEM(shape, F32)
    scratch = (
        [vm(*big), vm(*big)] + [vm(*one)] * 12
        + [vm(levels * tiles, LANES), pltpu.VMEM((tiles, LANES), jnp.int32), vm(tiles, LANES), vm(tiles, LANES)]
        + [vm(bricks * per, LANES), vm(bricks * per, LANES), vm(levels * tiles, LANES)]
        + [pltpu.VMEM((tiles, LANES), jnp.int32), vm(tiles, LANES), vm(bricks, LANES)]
        + [pltpu.VMEM((ROWS // 2 * levels, 4 * LANES), BF16), vm(ROWS * levels, 2 * LANES)]
        + [vm(q_rows, LANES), vm(q_rows, LANES), vm(3, q_one_rows, LANES)]
        + [vm(2, levels * 8, LANES), vm(2, levels * 8, LANES), vm(3, levels, LANES), vm(3, levels, LANES)]
        + [vm(q_rows, LANES)] * 4 + [vm(levels * 8, LANES)] * 4
        + [vm(3, q_one_rows, LANES), vm(3, q_one_rows, LANES), vm(3, levels, LANES), vm(3, levels, LANES)]
        + [vm(q_rows, LANES), vm(q_one_rows, LANES)]
        + [pltpu.SemaphoreType.DMA((9,)), pltpu.SemaphoreType.DMA((3,))]
        + [pltpu.SemaphoreType.DMA] * 5
        + [pltpu.SemaphoreType.DMA((18,)), pltpu.SemaphoreType.DMA((18,)), pltpu.SemaphoreType.REGULAR]
    )
    field, force, res = pl.pallas_call(
        functools.partial(window_kernel, n_lon, n_lat, levels),
        out_shape=(
            jax.ShapeDtypeStruct(big, F32), jax.ShapeDtypeStruct(one, F32), jax.ShapeDtypeStruct((tiles, LANES), F32),
        ),
        in_specs=[hbm] * 9,
        out_specs=(hbm,) * 3,
        scratch_shapes=scratch,
        compiler_params=pltpu.CompilerParams(collective_id=0, has_side_effects=True, vmem_limit_bytes=62 << 20),
        name="window",
    )(
        concentration.reshape(big), adjoint.reshape(big), wind_east.reshape(one), wind_north.reshape(one),
        mixing.reshape(one), sound_col.reshape(tiles, LANES), kernel.reshape(levels * tiles, LANES),
        observed.reshape(tiles, LANES), obs_error.reshape(tiles, LANES),
    )
    parts = levels // COMBINE
    out, residual = pl.pallas_call(
        functools.partial(add_kernel, levels),
        out_shape=(jax.ShapeDtypeStruct(big, F32), jax.ShapeDtypeStruct((tiles, LANES), F32)),
        in_specs=[hbm] * 3,
        out_specs=(hbm, hbm),
        scratch_shapes=[
            vm(*big), vm(*one), vm(tiles, LANES),
            pltpu.SemaphoreType.DMA((parts,)), pltpu.SemaphoreType.DMA((parts,)), pltpu.SemaphoreType.DMA((3,)),
        ],
        compiler_params=pltpu.CompilerParams(vmem_limit_bytes=62 << 20),
        name="combine",
    )(field, force, res)
    return out.reshape(adjoint.shape), residual.reshape(observed.shape)


def solution(mesh):
    in_specs = (
        P(None, None, "lat", "lon"),
        P(None, None, "lat", "lon"),
        P(None, "lat", "lon"),
        P(None, "lat", "lon"),
        P(None, "lat", "lon"),
        P(None, ("lon", "lat"), None),
        P(None, ("lon", "lat"), None),
        P(None, ("lon", "lat"), None),
        P(None, ("lon", "lat"), None),
    )
    out_specs = (P(None, None, "lat", "lon"), P(None, ("lon", "lat"), None))
    return jax.shard_map(
        functools.partial(per_device, mesh.shape["lon"], mesh.shape["lat"]),
        mesh=mesh, in_specs=in_specs, out_specs=out_specs, check_vma=False,
    )
```

```python
import functools

import jax
import jax.numpy as jnp
from jax import lax
from jax.experimental import pallas as pl
from jax.experimental.pallas import tpu as pltpu
from jax.sharding import PartitionSpec as P

MESH = pl.DeviceIdType.MESH
LANES = 128
ROWS = 16
TRACERS = 8
BLOCK = TRACERS * ROWS
COMBINE = 8
UNROLL = 8
F32 = jnp.float32
BF16 = jnp.bfloat16


def lane_ids(rows):
    return lax.broadcasted_iota(jnp.int32, (rows, LANES), 1)


def row_ids(rows):
    return lax.broadcasted_iota(jnp.int32, (rows, LANES), 0)


def swap_blocks(v, lane):
    low = lane < 64
    even = (lane // 32) % 2 == 0
    out = []
    first = [None] * 4
    for b in range(2):
        first[b] = jnp.where(low, v[b], pltpu.roll(v[2 + b], 64, 1))
        first[2 + b] = jnp.where(low, pltpu.roll(v[b], 64, 1), v[2 + b])
    for h in range(2):
        a, b = first[2 * h], first[2 * h + 1]
        out.append(jnp.where(even, a, pltpu.roll(b, 32, 1)))
        out.append(jnp.where(even, pltpu.roll(a, 96, 1), b))
    return out


def pack_lon(src, blocks, dst):
    pair = ((lane_ids(8) + 127) % 128) // 2
    bits = [lax.bitwise_and(pair, 1 << b) != 0 for b in range(6)]

    def tree(parts, level):
        while len(parts) > 1:
            parts = [jnp.where(bits[level], parts[2 * i + 1], parts[2 * i]) for i in range(len(parts) // 2)]
            level += 1
        return parts[0]

    def group(g, count):
        blocks_out = []
        for kk in range(count):
            parts = []
            for j in range(16):
                v = src[pl.ds(pl.multiple_of((g * 4 + kk) * BLOCK + j * 8, 8), 8), :]
                parts.append(pltpu.roll(v, (2 * (kk * 16 + j) + 2) % LANES, 1))
            blocks_out.append(tree(parts, 0))
        blocks_out = (blocks_out * 4)[:4] if count < 4 else blocks_out
        dst[pl.ds(pl.multiple_of(g * 8, 8), 8), :] = tree(blocks_out, 4)

    def body(g, c):
        group(g, 4)
        return c

    lax.fori_loop(0, blocks // 4, body, 0, unroll=3)
    if blocks % 4:
        group(blocks // 4, blocks % 4)


def pack_lat(src, blocks, row, dst):
    def body(k, c):
        dst[pl.ds(pl.multiple_of(k * 8, 8), 8), :] = src[pl.ds(k * BLOCK + row, 8, stride=ROWS), :]
        return c

    lax.fori_loop(0, blocks, body, 0, unroll=3)


def merge_lon(west, east, groups, dst):
    odd = lane_ids(8) % 2 == 1

    def body(g, c):
        rows = pl.ds(pl.multiple_of(g * 8, 8), 8)
        dst[rows, :] = jnp.where(odd, west[rows, :], pltpu.roll(east[rows, :], 126, 1))
        return c

    lax.fori_loop(0, groups, body, 0)


def outer_columns(merged, block, j):
    rows = pl.ds(pl.multiple_of((block // 4) * 8, 8), 8)
    v = merged[rows, :]
    slot = lax.rem(block, 4) * 16 + 2 * j
    return jnp.concatenate(
        [pltpu.roll(v, LANES - 1 - 2 * slot, 1), pltpu.roll(v, LANES - 3 - 2 * slot, 1)], axis=0
    )


def transport(field, levels, which, merged, south, north, coef):
    lane = lane_ids(ROWS)
    row = row_ids(ROWS)
    first_lane, last_lane = lane == 0, lane == LANES - 1
    first_row, last_row = row == 0, row == ROWS - 1
    c0, ce, cw, cn, cs, ca, cg = coef

    def stencil(block, j, level, above, v, east, west):
        at = pl.multiple_of(block * BLOCK + j * ROWS, 8)
        cols = outer_columns(merged, block, j)
        edge = block * 8 + j
        lo = jnp.broadcast_to(south[pl.ds(edge, 1), :], (ROWS, LANES))
        hi = jnp.broadcast_to(north[pl.ds(edge, 1), :], (ROWS, LANES))
        east = jnp.where(last_lane, cols, east)
        west = jnp.where(first_lane, cols, west)
        up = jnp.where(last_row, hi, pltpu.roll(v, ROWS - 1, 0))
        dn = jnp.where(first_row, lo, pltpu.roll(v, 1, 0))
        new = level[0] * v + level[1] * east + level[2] * west + level[3] * up + level[4] * dn + level[5] * above
        field[pl.ds(at, ROWS), :] = new
        return new

    def down(block, j, level, above):
        v = field[pl.ds(pl.multiple_of(block * BLOCK + j * ROWS, 8), ROWS), :]
        return stencil(block, j, level, above, v, pltpu.roll(v, LANES - 1, 1), pltpu.roll(v, 1, 1))

    def at_level(k, refs):
        rows = pl.ds(pl.multiple_of(k * ROWS, ROWS), ROWS)
        return [ref[rows, :] for ref in refs]

    if which is not None:

        count = len(which)
        source = lax.broadcasted_iota(jnp.int32, (2 * LANES, 2 * LANES), 0) % LANES
        target = lax.broadcasted_iota(jnp.int32, (2 * LANES, 2 * LANES), 1)
        shift = jnp.where(target < LANES, target + 1, target - LANES - 1)
        shift = jnp.where(source == shift, 1.0, 0.0).astype(BF16)

        def down_body(i, carry):
            values, sides = [], []
            for u in range(UNROLL):
                k = i * UNROLL + u
                v = field[pl.ds(pl.multiple_of(k * BLOCK + which[0] * ROWS, 8), count * ROWS), :]
                high = v.astype(BF16)
                low = (v - high.astype(F32)).astype(BF16)
                values.append(v)
                sides.append(jnp.dot(jnp.concatenate([high, low], axis=1), shift, preferred_element_type=F32))
            for u in range(UNROLL):
                k = i * UNROLL + u
                level = at_level(k, (c0, ce, cw, cn, cs, ca))
                new = []
                for n, t in enumerate(which):
                    rows = slice(n * ROWS, (n + 1) * ROWS)
                    new.append(stencil(
                        k, t, level, carry[n], values[u][rows], sides[u][rows, :LANES], sides[u][rows, LANES:]
                    ))
                carry = tuple(new)
            return carry

        zero = jnp.zeros((ROWS, LANES), F32)
        last = lax.fori_loop(0, levels // UNROLL, down_body, (zero,) * count)

        def up_body(i, carry):
            k = levels - 2 - i
            g = at_level(k, (cg,))[0]
            out = []
            for t, below in zip(which, carry):
                rows = pl.ds(pl.multiple_of(k * BLOCK + t * ROWS, 8), ROWS)
                new = field[rows, :] + g * below
                field[rows, :] = new
                out.append(new)
            return tuple(out)

        lax.fori_loop(0, levels - 1, up_body, last, unroll=4)
    else:

        def down_one(a, carry):
            for b in range(8):
                carry = down(a, b, at_level(a * 8 + b, (c0, ce, cw, cn, cs, ca)), carry)
            return carry

        last = lax.fori_loop(0, levels // 8, down_one, jnp.zeros((ROWS, LANES), F32))

        def up_one(i, carry):
            for b in range(8):
                k = levels - 1 - (i * 8 + b)
                rows = pl.ds(pl.multiple_of(k * ROWS, ROWS), ROWS)
                carry = field[rows, :] + cg[rows, :] * carry
                field[rows, :] = carry
            return carry

        lax.fori_loop(0, levels // 8, up_one, jnp.zeros((ROWS, LANES), F32))


def window_kernel(
    n_lon, n_lat, levels,
    conc_hbm, adj_hbm, we_hbm, wn_hbm, mix_hbm, col_hbm, kern_hbm, obs_hbm, err_hbm,
    adj_out, force_out, res_out,
    field, conc, we, wn, mix, prof, force, c0, ce, cw, cn, cs, ca, cg,
    kv, colv, obsv, errv, sendb, recvb, kn, coln, wres, resb,
    prof2, total,
    q_adj0, q_adj1, q_one, lat_a, lat_b, lat_one_a, lat_one_b,
    w_adj0, e_adj0, w_adj1, e_adj1, s_adj0, n_adj0, s_adj1, n_adj1,
    w_one, e_one, s_one, n_one, m_adj, m_one,
    load_sem, out_sem, a2a_send, a2a_recv, res_send, res_recv, self_sem, halo_send, halo_recv, stage_sem,
):
    lon, lat = lax.axis_index("lon"), lax.axis_index("lat")
    bricks = n_lon * n_lat
    me = lon * n_lat + lat
    per = levels // 4 + 1
    tiles = bricks // 4
    groups = tiles // 8

    loads = [
        (kern_hbm, kv), (col_hbm, colv), (obs_hbm, obsv), (err_hbm, errv), (we_hbm, we), (wn_hbm, wn),
        (adj_hbm, field), (mix_hbm, mix), (conc_hbm, conc),
    ]
    loads = [pltpu.make_async_copy(a, b, load_sem.at[i]) for i, (a, b) in enumerate(loads)]
    for copy in loads:
        copy.start()

    barrier = pltpu.get_barrier_semaphore()
    for d in range(1, n_lat):
        pl.semaphore_signal(barrier, inc=1, device_id=(lon, lax.rem(lat + d, n_lat)), device_id_type=MESH)
    for d in range(1, n_lon):
        pl.semaphore_signal(barrier, inc=1, device_id=(lax.rem(lon + d, n_lon), lat), device_id_type=MESH)

    lane8 = lane_ids(8)

    def pack_soundings():
        for i in range(4):
            loads[i].wait()

        def pack_rows(kk, c, v):
            y = swap_blocks(v, lane8)
            for m in range(4):
                sendb[pl.ds((c * 32 + m) * per + kk, 8, stride=4 * per), :] = y[m]

        def pack_body(kk, carry):
            for c in range(groups):
                pack_rows(kk, c, [kv[pl.ds(pl.multiple_of((kk * 4 + q) * tiles + c * 8, 8), 8), :] for q in range(4)])
            return carry

        lax.fori_loop(0, levels // 4, pack_body, 0, unroll=3)
        for c in range(groups):
            rows = pl.ds(c * 8, 8)
            e = errv[rows, :]
            pack_rows(levels // 4, c, [colv[rows, :].astype(F32), obsv[rows, :], e, e])


    def pack_halos():
        loads[4].wait()
        loads[5].wait()
        pack_lon(we, levels // 8, q_one.at[0])
        pack_lat(wn, levels // 8, ROWS - 1, lat_one_a.at[0])
        loads[6].wait()
        pack_lon(field, levels, q_adj0)
        pack_lat(field, levels, ROWS - 1, lat_a.at[0])
        pack_lat(field, levels, 0, lat_b.at[0])


    def enter():
        pl.semaphore_wait(barrier, n_lon + n_lat - 2)
        for d in range(1, n_lat):
            pl.semaphore_signal(stage_sem, inc=1, device_id=(lon, lax.rem(lat + d, n_lat)), device_id_type=MESH)
        pl.semaphore_wait(stage_sem, n_lat - 1)

    east = (lax.rem(lon + 1, n_lon), lat)
    west = (lax.rem(lon + n_lon - 1, n_lon), lat)
    north = (lon, lax.rem(lat + 1, n_lat))
    south = (lon, lax.rem(lat + n_lat - 1, n_lat))

    def remote(src, dst, index, device):
        return pltpu.make_async_remote_copy(
            src, dst, halo_send.at[index], halo_recv.at[index], device_id=device, device_id_type=MESH
        )

    def exchange(first, q, top, bottom, w, e, s, n):
        copies = [
            remote(top, s, first, north), remote(bottom, n, first + 1, south),
            remote(q, w, first + 2, east), remote(q, e, first + 3, west),
        ]
        for copy in copies:
            copy.start()
        return copies

    def land(copies):
        for copy in copies:
            copy.wait()

    def send_halos():
        wind_copies = [
            remote(q_one.at[0], w_one.at[0], 0, east), remote(lat_one_a.at[0], s_one.at[0], 1, north),
        ]
        for copy in wind_copies:
            copy.start()
        halo = exchange(2, q_adj0, lat_a.at[0], lat_b.at[0], w_adj0, e_adj0, s_adj0, n_adj0)
        return wind_copies, halo

    lons = [lax.rem(lon + d, n_lon) for d in range(n_lon)]
    lats = [lax.rem(lat + d, n_lat) for d in range(n_lat)]
    peers = []
    for i in range(1, bricks):
        d = (i * 37) % bricks
        tl, ta = lons[d // n_lat], lats[d % n_lat]
        peers.append((tl, ta, tl * n_lat + ta))

    def send_soundings(which):
        for tl, ta, t in which:
            pltpu.make_async_remote_copy(
                sendb.at[pl.ds(t * per, per)], recvb.at[pl.ds(me * per, per)], a2a_send, a2a_recv,
                device_id=(tl, ta), device_id_type=MESH,
            ).start()

    def sum_tracers():
        loads[8].wait()

        def tracer_sum(k, c):
            total = conc[pl.ds(pl.multiple_of(k * BLOCK, 8), ROWS), :]
            for t in range(1, TRACERS):
                total = total + conc[pl.ds(pl.multiple_of(k * BLOCK + t * ROWS, 8), ROWS), :]
            prof[pl.ds(pl.multiple_of(k * ROWS, 8), ROWS), :] = total
            return c

        lax.fori_loop(0, levels, tracer_sum, 0, unroll=2)

    own = pltpu.make_async_copy(sendb.at[pl.ds(me * per, per)], recvb.at[pl.ds(me * per, per)], self_sem)
    early = bricks * 3 // 8
    pack_soundings()
    enter()
    send_soundings(peers[:early])
    pack_halos()
    wind_copies, halo = send_halos()
    sum_tracers()
    loads[7].wait()

    land(wind_copies)
    lane = lane_ids(ROWS)
    row = row_ids(ROWS)
    merge_lon(w_one.at[0], w_one.at[0], (levels // 8 + 3) // 4, m_one)
    southmost = lat == 0
    northmost = lat == n_lat - 1
    open_north = jnp.logical_not(jnp.logical_and(row == ROWS - 1, northmost)).astype(F32)
    open_south = jnp.where(southmost, 0.0, 1.0)

    def coefficients(a, carry):
        above, factor = carry
        for b in range(8):
            k = a * 8 + b
            rows = pl.ds(pl.multiple_of(k * ROWS, ROWS), ROWS)
            u, n = we[rows, :], wn[rows, :]
            cols = outer_columns(m_one, a, b)
            u_west = jnp.where(lane == 0, cols, pltpu.roll(u, 1, 1))
            edge = jnp.broadcast_to(s_one[0, pl.ds(k, 1), :], (ROWS, LANES)) * open_south
            n_south = jnp.where(row == 0, edge, pltpu.roll(n, 1, 0))
            ep, wm = jnp.maximum(u, 0.0), jnp.minimum(u_west, 0.0)
            up, sm = jnp.maximum(n, 0.0), jnp.minimum(n_south, 0.0)
            below = mix[rows, :] * jnp.where(k < levels - 1, 1.0, 0.0)
            inv = 1.0 / (1.0 + below + above - above * factor)
            c0[rows, :] = (1.0 - ep + wm - up + sm) * inv
            ce[rows, :] = ep * inv
            cw[rows, :] = -wm * inv
            cn[rows, :] = up * open_north * inv
            cs[rows, :] = -sm * inv
            ca[rows, :] = above * inv
            factor = below * inv
            cg[rows, :] = factor
            above = below
        return above, factor

    zero = jnp.zeros((ROWS, LANES), F32)
    lax.fori_loop(0, levels // 8, coefficients, (zero, zero))
    coef = (c0, ce, cw, cn, cs, ca, cg)

    land(halo)
    send_soundings(peers[early:])
    own.start()
    merge_lon(w_adj0, e_adj0, levels // 4, m_adj)
    transport(field, levels, range(TRACERS), m_adj, s_adj0, n_adj0, coef)
    pack_lon(field, levels, q_adj1)
    pack_lat(field, levels, ROWS - 1, lat_a.at[1])
    pack_lat(field, levels, 0, lat_b.at[1])
    adj_halo = exchange(6, q_adj1, lat_a.at[1], lat_b.at[1], w_adj1, e_adj1, s_adj1, n_adj1)

    own.wait()
    rest = pl.ds(0, (bricks - 1) * per)
    pltpu.make_async_copy(recvb.at[rest], recvb.at[rest], a2a_recv).wait()

    def unpack(kk, c):
        z = [recvb[pl.ds((c * 32 + m) * per + kk, 8, stride=4 * per), :] for m in range(4)]
        return swap_blocks(z, lane8)

    def unpack_body(kk, carry):
        for c in range(groups):
            v = unpack(kk, c)
            for q in range(4):
                kn[pl.ds(pl.multiple_of((kk * 4 + q) * tiles + c * 8, 8), 8), :] = v[q]
        return carry

    lax.fori_loop(0, levels // 4, unpack_body, 0, unroll=3)
    for c in range(groups):
        rows = pl.ds(c * 8, 8)
        aux = unpack(levels // 4, c)
        coln[rows, :] = aux[0].astype(jnp.int32)
        obsv[rows, :] = aux[1]
        errv[rows, :] = aux[2]

    for r in range(ROWS):
        v = prof[pl.ds(r, levels, stride=ROWS), :]
        high = v.astype(BF16)
        rows, at = pl.ds(r // 2 * levels, levels), r % 2 * LANES
        prof2[rows, pl.ds(at, LANES)] = high
        prof2[rows, pl.ds(2 * LANES + at, LANES)] = (v - high.astype(F32)).astype(BF16)

    cell = lax.broadcasted_iota(jnp.int32, (2 * LANES, 2 * LANES), 0)

    def pair_of(ref, i):
        return jnp.concatenate([ref[pl.ds(2 * i, 1), :], ref[pl.ds(2 * i + 1, 1), :]], axis=1)

    def soundings(i, carry):
        col, obs, err = pair_of(coln, i), pair_of(obsv, i), pair_of(errv, i)
        half = lax.shift_right_arithmetic(col, 8)
        hot = jnp.where(lax.bitwise_and(col, 2 * LANES - 1) == cell, 1.0, 0.0).astype(BF16)
        g = jnp.dot(prof2[...], jnp.concatenate([hot, hot], axis=0), preferred_element_type=F32)
        parts = [g[r * levels : (r + 1) * levels] for r in range(ROWS // 2)]
        for b in range(3):
            bit = lax.bitwise_and(half, 1 << b) != 0
            parts = [jnp.where(bit, parts[2 * j + 1], parts[2 * j]) for j in range(len(parts) // 2)]
        w = jnp.concatenate(
            [kn[pl.ds(2 * i, levels, stride=tiles), :], kn[pl.ds(2 * i + 1, levels, stride=tiles), :]], axis=1
        )
        modelled = jnp.sum(w * parts[0], axis=0, keepdims=True)
        res = jnp.where(col >= 0, (modelled - obs) / err, 0.0)
        wres[pl.ds(2 * i, 1), :] = res[:, :LANES]
        wres[pl.ds(2 * i + 1, 1), :] = res[:, LANES:]
        w = w * (res / err)
        high = w.astype(BF16).astype(F32)
        low = w - high
        lhs = jnp.concatenate(
            [jnp.where(half == r, v, 0.0) for v in (high, low) for r in range(ROWS // 2)], axis=0
        ).astype(BF16)
        total[...] += lax.dot_general(lhs, hot, (((1,), (1,)), ((), ())), preferred_element_type=F32)
        return carry

    total[...] = jnp.zeros_like(total)
    lax.fori_loop(0, tiles // 2, soundings, 0, unroll=4)

    for r in range(ROWS):
        lanes = pl.ds(r % 2 * LANES, LANES)
        at = r // 2 * levels
        force[pl.ds(r, levels, stride=ROWS), :] = (
            total[pl.ds(at, levels), lanes] + total[pl.ds(levels * ROWS // 2 + at, levels), lanes]
        )

    def send_force(step):
        pack_lon(force, levels // 8, q_one.at[step])
        pack_lat(force, levels // 8, ROWS - 1, lat_one_a.at[step])
        pack_lat(force, levels // 8, 0, lat_one_b.at[step])
        return exchange(
            6 + 4 * step, q_one.at[step], lat_one_a.at[step], lat_one_b.at[step],
            w_one.at[step], e_one.at[step], s_one.at[step], n_one.at[step],
        )

    def step_force(step, halo):
        land(halo)
        merge_lon(w_one.at[step], e_one.at[step], (levels // 8 + 3) // 4, m_one)
        transport(force, levels, None, m_one, s_one.at[step], n_one.at[step], coef)

    halo = send_force(1)
    land(adj_halo)
    merge_lon(w_adj1, e_adj1, levels // 4, m_adj)
    transport(field, levels, range(0, TRACERS // 2), m_adj, s_adj1, n_adj1, coef)
    step_force(1, halo)
    halo = send_force(2)
    for tl, ta, t in peers:
        pltpu.make_async_remote_copy(
            wres.at[pl.ds(t // 4, 1)], resb.at[pl.ds(me, 1)], res_send, res_recv,
            device_id=(tl, ta), device_id_type=MESH,
        ).start()
    own_res = pltpu.make_async_copy(wres.at[pl.ds(me // 4, 1)], resb.at[pl.ds(me, 1)], self_sem)
    own_res.start()

    transport(field, levels, range(TRACERS // 2, TRACERS), m_adj, s_adj1, n_adj1, coef)
    adj_copy = pltpu.make_async_copy(field, adj_out, out_sem.at[0])
    adj_copy.start()
    step_force(2, halo)
    force_copy = pltpu.make_async_copy(force, force_out, out_sem.at[1])
    force_copy.start()

    own_res.wait()
    rest_res = pl.ds(0, bricks - 1)
    pltpu.make_async_copy(resb.at[rest_res], resb.at[rest_res], res_recv).wait()
    mine_block = lax.rem(me, 4)
    for g in range(groups):
        mine = jnp.zeros((8, LANES), F32)
        for m in range(4):
            v = resb[pl.ds(g * 32 + m, 8, stride=4), :]
            shift = lax.rem((m - mine_block + 4) * 32, LANES)
            mine = jnp.where(lane8 // 32 == m, pltpu.roll(v, shift, 1), mine)
        errv[pl.ds(g * 8, 8), :] = mine
    res_copy = pltpu.make_async_copy(errv, res_out, out_sem.at[2])
    res_copy.start()

    pltpu.make_async_copy(recvb.at[rest], recvb.at[rest], a2a_send).wait()
    pltpu.make_async_copy(resb.at[rest_res], resb.at[rest_res], res_send).wait()
    adj_copy.wait()
    force_copy.wait()
    res_copy.wait()


def add_kernel(levels, field, force, res, out, res_out, buf, one, rows_buf, in_sem, out_sem, aux_sem):
    parts = levels // COMBINE
    rows = COMBINE * BLOCK
    aux = [
        pltpu.make_async_copy(force, one, aux_sem.at[0]), pltpu.make_async_copy(res, rows_buf, aux_sem.at[1]),
        pltpu.make_async_copy(rows_buf, res_out, aux_sem.at[2]),
    ]
    aux[0].start()
    reads, writes = [], []
    for p in range(parts):
        at = pl.ds(p * rows, rows)
        reads.append(pltpu.make_async_copy(field.at[at], buf.at[at], in_sem.at[p]))
        writes.append(pltpu.make_async_copy(buf.at[at], out.at[at], out_sem.at[p]))
        reads[p].start()
    aux[1].start()
    aux[0].wait()
    for p in range(parts):
        reads[p].wait()

        def body(k, c):
            add = one[pl.ds(pl.multiple_of(k * ROWS, ROWS), ROWS), :]
            for t in range(TRACERS):
                at = pl.ds(pl.multiple_of(k * BLOCK + t * ROWS, ROWS), ROWS)
                buf[at, :] = buf[at, :] + add
            return c

        lax.fori_loop(p * COMBINE, (p + 1) * COMBINE, body, 0, unroll=4)
        writes[p].start()
        if p == 0:
            aux[1].wait()
            aux[2].start()
    for copy in writes:
        copy.wait()
    aux[2].wait()


def per_device(n_lon, n_lat, concentration, adjoint, wind_east, wind_north, mixing, sound_col, kernel, observed, obs_error):
    levels, tracers, row_count, col_count = adjoint.shape
    bricks = n_lon * n_lat
    slots = sound_col.shape[2]
    tiles = slots // LANES
    per = levels // 4 + 1
    big, one = (levels * BLOCK, LANES), (levels * ROWS, LANES)
    q_rows, q_one_rows = levels // 4 * 8, (levels // 8 + 3) // 4 * 8
    hbm = pl.BlockSpec(memory_space=pl.ANY)
    vm = lambda *shape: pltpu.VMEM(shape, F32)
    scratch = (
        [vm(*big), vm(*big)] + [vm(*one)] * 12
        + [vm(levels * tiles, LANES), pltpu.VMEM((tiles, LANES), jnp.int32), vm(tiles, LANES), vm(tiles, LANES)]
        + [vm(bricks * per, LANES), vm(bricks * per, LANES), vm(levels * tiles, LANES)]
        + [pltpu.VMEM((tiles, LANES), jnp.int32), vm(tiles, LANES), vm(bricks, LANES)]
        + [pltpu.VMEM((ROWS // 2 * levels, 4 * LANES), BF16), vm(ROWS * levels, 2 * LANES)]
        + [vm(q_rows, LANES), vm(q_rows, LANES), vm(3, q_one_rows, LANES)]
        + [vm(2, levels * 8, LANES), vm(2, levels * 8, LANES), vm(3, levels, LANES), vm(3, levels, LANES)]
        + [vm(q_rows, LANES)] * 4 + [vm(levels * 8, LANES)] * 4
        + [vm(3, q_one_rows, LANES), vm(3, q_one_rows, LANES), vm(3, levels, LANES), vm(3, levels, LANES)]
        + [vm(q_rows, LANES), vm(q_one_rows, LANES)]
        + [pltpu.SemaphoreType.DMA((9,)), pltpu.SemaphoreType.DMA((3,))]
        + [pltpu.SemaphoreType.DMA] * 5
        + [pltpu.SemaphoreType.DMA((18,)), pltpu.SemaphoreType.DMA((18,)), pltpu.SemaphoreType.REGULAR]
    )
    field, force, res = pl.pallas_call(
        functools.partial(window_kernel, n_lon, n_lat, levels),
        out_shape=(
            jax.ShapeDtypeStruct(big, F32), jax.ShapeDtypeStruct(one, F32), jax.ShapeDtypeStruct((tiles, LANES), F32),
        ),
        in_specs=[hbm] * 9,
        out_specs=(hbm,) * 3,
        scratch_shapes=scratch,
        compiler_params=pltpu.CompilerParams(collective_id=0, has_side_effects=True, vmem_limit_bytes=62 << 20),
        name="window",
    )(
        concentration.reshape(big), adjoint.reshape(big), wind_east.reshape(one), wind_north.reshape(one),
        mixing.reshape(one), sound_col.reshape(tiles, LANES), kernel.reshape(levels * tiles, LANES),
        observed.reshape(tiles, LANES), obs_error.reshape(tiles, LANES),
    )
    parts = levels // COMBINE
    out, residual = pl.pallas_call(
        functools.partial(add_kernel, levels),
        out_shape=(jax.ShapeDtypeStruct(big, F32), jax.ShapeDtypeStruct((tiles, LANES), F32)),
        in_specs=[hbm] * 3,
        out_specs=(hbm, hbm),
        scratch_shapes=[
            vm(*big), vm(*one), vm(tiles, LANES),
            pltpu.SemaphoreType.DMA((parts,)), pltpu.SemaphoreType.DMA((parts,)), pltpu.SemaphoreType.DMA((3,)),
        ],
        compiler_params=pltpu.CompilerParams(vmem_limit_bytes=62 << 20),
        name="combine",
    )(field, force, res)
    return out.reshape(adjoint.shape), residual.reshape(observed.shape)


def solution(mesh):
    in_specs = (
        P(None, None, "lat", "lon"),
        P(None, None, "lat", "lon"),
        P(None, "lat", "lon"),
        P(None, "lat", "lon"),
        P(None, "lat", "lon"),
        P(None, ("lon", "lat"), None),
        P(None, ("lon", "lat"), None),
        P(None, ("lon", "lat"), None),
        P(None, ("lon", "lat"), None),
    )
    out_specs = (P(None, None, "lat", "lon"), P(None, ("lon", "lat"), None))
    return jax.shard_map(
        functools.partial(per_device, mesh.shape["lon"], mesh.shape["lat"]),
        mesh=mesh, in_specs=in_specs, out_specs=out_specs, check_vma=False,
    )
```
